32 devices in a mesh: seq: 2 (over core), expert: 16 (over z, y, x).
Axes of the slice: x: 2, y: 2, z: 4, core: 2. Of those that a mesh axis runs over, the one named last changes fastest.
Arguments:
- tokens: bfloat16 [4096, 4096], P(('seq', 'expert')), may hold values from -6 to 6
- routes: int32 [4096, 2], P(('seq', 'expert')), may hold values from 0 to 15, all different within a row; in each aligned block of 128 rows (0 to 127, 128 to 255, ...) at most 24 rows name the same one
- route_probs: float32 [4096, 2], P(('seq', 'expert')), may hold values from 0.25 to 1
- gate_weight: bfloat16 [16, 4096, 768], P('expert', None, 'seq'), may hold values from -0.09375 to 0.09375
- up_weight: bfloat16 [16, 4096, 768], P('expert', None, 'seq'), may hold values from -0.09375 to 0.09375
- down_weight: bfloat16 [16, 768, 4096], P('expert', 'seq'), may hold values from -0.21875 to 0.21875
- grad_out: bfloat16 [4096, 4096], P(('seq', 'expert')), may hold values from -3 to 3
Outputs:
- grad_tokens: bfloat16 [4096, 4096], P(('seq', 'expert'))
- grad_probs: bfloat16 [4096, 2], P(('seq', 'expert'))
The draws below stay inside these ranges and needn't reach their ends.
Inputs may be any that keep to these rules, and one draw needn't show every extreme that they name: `routes`: each token names 2 different experts. Among the tokens of one device no expert is named by more than 24 tokens, and in every draw some device names some expert exactly 24 times.
All inputs are finite; a program needn't handle non-finite values.
Results may differ from the reference program's by a relative error of at most 0.01.
Values may be sent and summed in bfloat16 or wider, within the bound.
A program may use at most 128 MiB of HBM per device.

```python
import math
import jax
import jax.numpy as jnp
import numpy as np
from jax import lax

D = 4096
H = 768
TOPK = 2
TOK_DEV = 128
EXPERTS = 16
CAP = 24
TOKENS = 4096
N_SEQ = 2
N_EXPERT = 16


def block_levels(stream_key, shape, split, least, top_value):
    loudness = 1.0
    for position, blocks in split:
        draws = jax.random.uniform(jax.random.fold_in(jax.random.fold_in(stream_key, 6), position), (blocks,), jnp.float32, least / len(split), top_value / len(split))
        loudness = loudness * jnp.repeat(jnp.exp(draws), shape[position] // blocks).reshape((-1,) + (1,) * (len(shape) - 1 - position))
    return loudness


def shared_out(stream_key, own, number, rows, number_of, top, reach, slope):
    sequence = jax.random.permutation(stream_key, number_of)
    packed, usual = load_shares(number_of, rows * top, reach, slope, True), load_shares(number_of, rows * top, reach, slope, False)
    places = jnp.arange(number_of)

    def named(lengths, rotation):
        used = int((lengths > 0).sum())
        fixed = max(1, used // 4)
        moved = fixed + (places - fixed + rotation * (used - fixed)) % max(1, number_of - fixed)
        return jnp.zeros((number_of,), jnp.int32).at[sequence[jnp.where(places < fixed, places, moved)]].set(jnp.asarray(lengths, jnp.int32))

    lengths = jnp.where(number % 4 == 0, named(packed, number // 4), named(usual, number - number // 4 - 1))
    mixed = jax.random.permutation(jax.random.fold_in(own, 3), number_of)
    donor, sink = mixed[0:number_of // 2 * 2:2], mixed[1:number_of // 2 * 2:2]
    margin = jnp.minimum(lengths[donor] - 1, reach - lengths[sink]) // 2
    margin = jnp.where((donor == sequence[0]) | (sink == sequence[0]) | (lengths[sink] == 0), 0, jnp.maximum(margin, 0))
    moved = jax.random.randint(jax.random.fold_in(own, 4), (number_of // 2,), 0, 1 << 20) % (margin + 1)
    lengths = lengths.at[donor].add(-moved).at[sink].add(moved)
    members = jnp.searchsorted(jnp.cumsum(lengths), jnp.arange(rows * top), side="right").astype(jnp.int32)
    grid = members.reshape(top, rows).T
    grid = grid[jax.random.permutation(jax.random.fold_in(own, 1), rows)]
    rotation = jax.random.randint(jax.random.fold_in(own, 2), (rows, 1), 0, top)
    return jnp.take_along_axis(grid, (jnp.arange(top)[None, :] + rotation) % top, axis=1)


def load_shares(amount, total, limit, slope, full):
    weights = [(1 << 20) // math.isqrt(standing ** slope) + 1 for standing in range(1, amount + 1)]
    largest = limit if full else min(limit, max(-(-total // amount), total * weights[0] // sum(weights)))
    least = 1 if total - largest >= amount - 1 else 0
    given, surplus = [largest] + [least] * (amount - 1), total - largest - least * (amount - 1)
    while surplus > 0:
        free = [i for i in range(1, amount) if given[i] < largest] or [i for i in range(1, amount) if given[i] < limit]
        mass, remaining = sum([weights[i] for i in free]), surplus
        for i in free:
            more = min(limit - given[i], max(1, remaining * weights[i] // mass), surplus)
            given[i] = given[i] + more
            surplus = surplus - more
    return np.array(given)


def gaussian(rng, extent, scale, bound, split=(), kind=jnp.bfloat16):
    entries = scale * jax.random.normal(rng, extent, jnp.float32)
    if split:
        entries = entries * block_levels(rng, extent, split, -0.22, 0.18)
    return jnp.clip(entries, -bound, bound).astype(kind)


def setup_inputs(seed: int = 0) -> dict:
    key_of = jax.random.split(jax.random.key(seed), 8)
    tokens = gaussian(key_of[0], (TOKENS, D), 1.0, 6.0, ((0, 32),))
    routes_keys = jax.random.split(jax.random.fold_in(key_of[1], 1), TOKENS // TOK_DEV)
    routes_turns = jax.random.permutation(jax.random.fold_in(key_of[1], 3), TOKENS // TOK_DEV)
    routes = jax.vmap(lambda own, number: shared_out(jax.random.fold_in(key_of[1], 2), own, number, TOK_DEV, EXPERTS, TOPK, CAP, 1))(routes_keys, routes_turns).reshape((TOKENS, TOPK))
    route_probs = jnp.clip(0.25 + 0.75 * jax.random.uniform(key_of[2], (TOKENS, TOPK), jnp.float32) ** block_levels(key_of[2], (TOKENS, TOPK), ((0, 32),), -0.2, 0.2), 0.25, 1.0)
    gate_weight = gaussian(key_of[3], (EXPERTS, D, H), D ** -0.5, 0.09375, ((0, 16), (2, 2)))
    up_weight = gaussian(key_of[4], (EXPERTS, D, H), D ** -0.5, 0.09375, ((0, 16), (2, 2)))
    down_weight = gaussian(key_of[5], (EXPERTS, H, D), H ** -0.5, 0.21875, ((0, 16), (1, 2)))
    grad_out = gaussian(key_of[6], (TOKENS, D), 0.5, 3.0, ((0, 32),))
    return dict(tokens=tokens, routes=routes, route_probs=route_probs, gate_weight=gate_weight, up_weight=up_weight, down_weight=down_weight, grad_out=grad_out)


def expert_terms(rows_in, rows_grad, gate_w, up_w, down_w):
    contract = (((1,), (1,)), ((), ()))
    gating = jnp.dot(rows_in, gate_w, preferred_element_type=jnp.float32)
    lifted = jnp.dot(rows_in, up_w, preferred_element_type=jnp.float32)
    sigmoid = jax.nn.sigmoid(gating)
    active = gating * sigmoid
    hidden = (active * lifted).astype(jnp.bfloat16)
    grad_hidden = lax.dot_general(rows_grad, down_w, contract, preferred_element_type=jnp.float32)
    grad_prob = jnp.sum(hidden.astype(jnp.float32) * grad_hidden, axis=1)
    slope_term = sigmoid * (1.0 + gating * (1.0 - sigmoid))
    grad_gate = (grad_hidden * lifted * slope_term).astype(jnp.bfloat16)
    grad_up = (grad_hidden * active).astype(jnp.bfloat16)
    grad_rows = lax.dot_general(grad_gate, gate_w, contract, preferred_element_type=jnp.float32)
    grad_rows = grad_rows + lax.dot_general(grad_up, up_w, contract, preferred_element_type=jnp.float32)
    return grad_rows, grad_prob


def reference(tokens, routes, route_probs, gate_weight, up_weight, down_weight, grad_out):
    total = TOKENS * TOPK
    chosen = routes.reshape(-1).astype(jnp.int32)
    ordering = jnp.argsort(chosen, stable=True).astype(jnp.int32)
    counts = jnp.zeros((EXPERTS,), jnp.int32).at[chosen].add(1)
    offsets = (jnp.cumsum(counts) - counts).astype(jnp.int32)
    row_limit = CAP * N_EXPERT * N_SEQ
    flat_probs = route_probs.reshape(-1)

    def per_expert(totals, expert):
        grad_acc, prob_acc = totals
        lanes = jnp.arange(row_limit, dtype=jnp.int32)
        flat_index = jnp.clip(offsets[expert] + lanes, 0, total - 1).astype(jnp.int32)
        is_live = lanes < counts[expert]
        assigned = ordering[flat_index]
        source = (assigned // TOPK).astype(jnp.int32)
        grad_rows, grad_prob = expert_terms(tokens[source], grad_out[source], gate_weight[expert], up_weight[expert], down_weight[expert])
        grad_rows = lax.optimization_barrier(grad_rows.astype(jnp.bfloat16))
        grad_prob = lax.optimization_barrier(grad_prob.astype(jnp.bfloat16))
        weighting = jnp.where(is_live, flat_probs[assigned], 0.0).astype(jnp.float32)
        grad_acc = grad_acc.at[source].add(weighting[:, None] * grad_rows.astype(jnp.float32))
        prob_acc = prob_acc.at[assigned].add(jnp.where(is_live, grad_prob.astype(jnp.float32), 0.0))
        return (grad_acc, prob_acc), None

    start = (jnp.zeros((TOKENS, D), jnp.float32), jnp.zeros((total,), jnp.float32))
    (grad_acc, prob_acc), _ = lax.scan(per_expert, start, jnp.arange(EXPERTS, dtype=jnp.int32))
    return grad_acc.astype(jnp.bfloat16), prob_acc.reshape(TOKENS, TOPK).astype(jnp.bfloat16)
```

```python
import jax
import jax.numpy as jnp
from jax import lax
from jax.experimental import pallas as pl
from jax.experimental.pallas import tpu as pltpu
from jax.sharding import PartitionSpec as P

CHUNKS = 2
PIECES = 4
PARTS = 2
LAYERS = 4
LANES = 128
I, O, FI, FO = range(4)
STEP = 512
MESH = pl.DeviceIdType.MESH
NT = (((1,), (1,)), ((), ()))


def dot(a, b):
    return jnp.dot(a, b, preferred_element_type=jnp.float32)


def dot_nt(a, b):
    return lax.dot_general(a, b, NT, preferred_element_type=jnp.float32)


def slots_of(routes, base, half, capacity):
    local = routes - base
    chosen = local.reshape(-1)
    order = jnp.arange(chosen.shape[0], dtype=jnp.int32)
    earlier = (chosen[:, None] == chosen[None, :]) & (order[None, :] < order[:, None])
    position = jnp.sum(earlier.astype(jnp.int32), axis=1).reshape(routes.shape)
    valid = (local >= 0) & (local < half)
    return jnp.where(valid, local * capacity + position, -1)


def dispatch_of(slots, count):
    lanes = jnp.arange(count, dtype=jnp.int32)[:, None, None]
    return jnp.any(lanes == slots[None], axis=2).astype(jnp.bfloat16)


def weighting_of(slots, probs, count):
    lanes = jnp.arange(count, dtype=jnp.int32)[None, None, :]
    full = jnp.sum(jnp.where(slots[:, :, None] == lanes, probs[:, :, None], 0.0), axis=1)
    high = lax.reduce_precision(full, 8, 7)
    return high.astype(jnp.bfloat16), (full - high).astype(jnp.bfloat16)


def combine(weighting, rows):
    return dot(weighting[0], rows) + dot(weighting[1], rows)


def pick(slots, values):
    lanes = jnp.arange(values.shape[0], dtype=jnp.int32)[None, None, :]
    return jnp.sum(jnp.where(slots[:, :, None] == lanes, values[None, None, :], 0.0), axis=2)


def front(rows_in, gates, ups):
    return [(dot(rows_in, g), dot(rows_in, u)) for g, u in zip(gates, ups)]


def middle(terms, rows_grad, downs):
    prob, grads = 0.0, []
    for (gating, lifted), d in zip(terms, downs):
        sigmoid = jax.nn.sigmoid(gating)
        active = gating * sigmoid
        hidden = (active * lifted).astype(jnp.bfloat16)
        grad_hidden = dot_nt(rows_grad, d)
        prob = prob + jnp.sum(hidden.astype(jnp.float32) * grad_hidden, axis=1)
        slope_term = sigmoid * (1.0 + gating * (1.0 - sigmoid))
        grads.append(
            (
                (grad_hidden * lifted * slope_term).astype(jnp.bfloat16),
                (grad_hidden * active).astype(jnp.bfloat16),
            )
        )
    return grads, prob


def back(grads, gates, ups, columns):
    total = 0.0
    for (gg, gu), g, u in zip(grads, gates, ups):
        total = total + dot_nt(gg, g[columns]) + dot_nt(gu, u[columns])
    return total.astype(jnp.bfloat16)


def halves_on_device(tokens, routes, route_probs, gate_weight, up_weight, down_weight, grad_out):
    tok_count, width = tokens.shape
    top_count = routes.shape[1]
    experts = lax.axis_size("expert")
    parts = lax.axis_size("seq")
    capacity = 3 * tok_count * top_count // (2 * experts)
    half = experts // 2
    count = half * capacity
    base = (lax.axis_index("expert") // half) * half
    swap = [(i, (i + half) % experts) for i in range(experts)]
    groups = [list(range(half)), list(range(half, experts))]

    def across(value):
        return lax.ppermute(value, "expert", swap)

    def exchange(value):
        value = value.reshape(half, capacity, -1)
        value = lax.all_to_all(
            value, "expert", split_axis=0, concat_axis=0, tiled=True, axis_index_groups=groups
        )
        return value.reshape(count, -1)

    far_routes, far_probs = across(routes), across(route_probs)
    far_tokens, far_grad = across(tokens), across(grad_out)

    gates, ups, downs = [gate_weight[0]], [up_weight[0]], [down_weight[0]]
    for shift in range(1, parts):
        turn = [(i, (i + shift) % parts) for i in range(parts)]
        gates.append(lax.ppermute(gate_weight[0], "seq", turn))
        ups.append(lax.ppermute(up_weight[0], "seq", turn))
        downs.append(lax.ppermute(down_weight[0], "seq", turn))

    near_slots = slots_of(routes, base, half, capacity)
    near_pick = dispatch_of(near_slots, count)
    near_in = exchange(dot(near_pick, tokens).astype(jnp.bfloat16))
    near_out = exchange(dot(near_pick, grad_out).astype(jnp.bfloat16))
    near_grads, near_prob = middle(front(near_in, gates, ups), near_out, downs)

    far_slots = slots_of(far_routes, base, half, capacity)
    far_pick = dispatch_of(far_slots, count)
    far_in = exchange(dot(far_pick, far_tokens).astype(jnp.bfloat16))
    far_terms = front(far_in, gates, ups)
    far_out = exchange(dot(far_pick, far_grad).astype(jnp.bfloat16))
    far_grads, far_prob = middle(far_terms, far_out, downs)

    near_weighting = weighting_of(near_slots, route_probs, count)
    far_weighting = weighting_of(far_slots, far_probs, count)

    size = width // CHUNKS
    spans = [slice(c * size, (c + 1) * size) for c in range(CHUNKS)]

    def send_back(grads, prob, span):
        rows = back(grads, gates, ups, span)
        if span.start == 0:
            column = jnp.broadcast_to(prob.astype(jnp.bfloat16)[:, None], (count, 128))
            rows = jnp.concatenate([rows, column], axis=1)
        return exchange(rows)

    returned = []
    for span in spans:
        rows = send_back(far_grads, far_prob, span)
        partial = combine(far_weighting, rows[:, :size]).astype(jnp.bfloat16)
        returned.append(across(partial))
        if span.start == 0:
            far_values = pick(far_slots, rows[:, size].astype(jnp.float32))
            far_values = across(far_values.astype(jnp.bfloat16))
    pieces = []
    for span, far_piece in zip(spans, returned):
        rows = send_back(near_grads, near_prob, span)
        near_piece = combine(near_weighting, rows[:, :size])
        pieces.append((near_piece + far_piece.astype(jnp.float32)).astype(jnp.bfloat16))
        if span.start == 0:
            near_values = pick(near_slots, rows[:, size].astype(jnp.float32))
    grad_probs = (near_values + far_values.astype(jnp.float32)).astype(jnp.bfloat16)
    return (jnp.concatenate(pieces, axis=1), grad_probs)


def fused_kernel(
    plane,
    table, tok_hbm, grad_hbm, gate_hbm, up_hbm, down_hbm,
    out, probs_out,
    own, picks, mats, far_table, land, gate_w, up_w, down_w, send, rows_in, acc, grad_hid, back_in,
    part_in,
    local_sem, w_send, w_recv, t_send, t_recv, x_send, x_recv, a_send, a_recv, b_send, b_recv,
    p_send, p_recv,
):
    width, capacity = own.shape[2], send.shape[2]
    full = land.shape[3]
    block = plane * capacity
    piece, part = width // PIECES, width // PARTS
    me = lax.axis_index("expert")
    core = lax.axis_index("seq")
    layer = me // plane
    col = me - layer * plane
    side = layer // (LAYERS // 2)
    inner = (layer == 1) | (layer == 2)
    outer = jnp.logical_not(inner)
    my_base, inner_base = layer * plane, (side + 1) * plane
    outer_base = side * (LAYERS - 1) * plane
    twin = {"seq": 1 - core}
    near_inner = {"expert": inner_base + col}
    near_outer = {"expert": outer_base + col}
    far_inner = {"expert": (2 - side) * plane + col}
    ring = [lax.rem(col + d, plane) for d in range(plane)]

    def remote(src, dst, ss, rs, device):
        return pltpu.make_async_remote_copy(
            src_ref=src, dst_ref=dst, send_sem=ss, recv_sem=rs,
            device_id=device, device_id_type=MESH,
        )

    def start(copies):
        for copy in copies:
            copy.start()

    def arrived(copies):
        for copy in copies:
            copy.wait_recv()

    def sent(copies):
        for copy in copies:
            copy.wait_send()

    weights = ((gate_hbm, gate_w), (up_hbm, up_w), (down_hbm, down_w))
    blocks = [
        pltpu.make_async_copy(src, own.at[i], local_sem.at[i])
        for i, src in enumerate((tok_hbm, grad_hbm))
    ]
    locals_ = [
        pltpu.make_async_copy(src.at[0], dst.at[0], local_sem.at[2 + i])
        for i, (src, dst) in enumerate(weights)
    ]
    start(blocks + locals_)

    barrier = pltpu.get_barrier_semaphore()

    def greet(device):
        pl.semaphore_signal(barrier, inc=1, device_id=device, device_id_type=MESH)

    greet(twin)
    for d in range(1, plane):
        greet({"expert": my_base + ring[d]})

    @pl.when(inner)
    def _():
        greet(far_inner)
        for d in range(plane):
            greet({"expert": outer_base + ring[d]})
        pl.semaphore_wait(barrier, 2 * plane + 1)

    @pl.when(outer)
    def _():
        for d in range(plane):
            greet({"expert": inner_base + ring[d]})
        pl.semaphore_wait(barrier, 2 * plane)

    def span(i):
        return pl.ds(i * part, part)

    def up_table(target, device):
        return remote(table, far_table.at[target], t_send.at[0], t_recv.at[target], device)

    def up_block(stream, i, target, device):
        source = (tok_hbm, grad_hbm)[stream]
        return remote(
            source.at[:, span(i)], land.at[target, stream, :, span(i)],
            x_send.at[0, stream, i], x_recv.at[target, stream, i], device,
        )

    def pass_table():
        return remote(far_table.at[0], far_table.at[2], t_send.at[1], t_recv.at[2], far_inner)

    def pass_block(stream, i):
        return remote(
            land.at[0, stream, :, span(i)], land.at[2, stream, :, span(i)],
            x_send.at[1, stream, i], x_recv.at[2, stream, i], far_inner,
        )

    def ups(target, device):
        return [up_table(target, device)] + [
            up_block(stream, i, target, device) for stream in range(2) for i in range(PARTS)
        ]

    @pl.when(inner)
    def _():
        start(ups(1, far_inner))

    @pl.when(outer)
    def _():
        start(ups(0, near_inner))

    swaps = [
        remote(src.at[0], dst.at[1], w_send.at[i], w_recv.at[i], twin)
        for i, (src, dst) in enumerate(weights)
    ]
    start(swaps)

    def tables(label, values, first, second, amount):
        count = amount * capacity
        p = lax.broadcasted_iota(jnp.int32, (amount, LANES), 0)
        expert = jnp.where(p < plane, first + p, second + p - plane).astype(jnp.float32)
        named = [jnp.where(values[k : k + 1] == expert, 1.0, 0.0) for k in range(2)]
        before = lax.broadcasted_iota(jnp.int32, (LANES, LANES), 0)
        after = lax.broadcasted_iota(jnp.int32, (LANES, LANES), 1)
        lower = jnp.where(before < after, 1.0, 0.0).astype(jnp.bfloat16)
        eye = jnp.where(before == after, 1.0, 0.0).astype(jnp.bfloat16)
        position = dot((named[0] + named[1]).astype(jnp.bfloat16), lower)
        place = lax.broadcasted_iota(jnp.int32, (amount, capacity, LANES), 1).astype(jnp.float32)
        hit = jnp.where(position[:, None, :] == place, 1.0, 0.0)
        chosen = [(hit * n[:, None, :]).reshape(count, LANES) for n in named]
        picks[label, :count] = (chosen[0] + chosen[1]).astype(jnp.bfloat16)
        weight = chosen[0] * values[2:3] + chosen[1] * values[3:4]
        high = weight.astype(jnp.bfloat16)
        low = (weight - high.astype(jnp.float32)).astype(jnp.bfloat16)
        for i, value in enumerate((high, low, *(c.astype(jnp.bfloat16) for c in chosen))):
            mats[label, i, :, :count] = dot_nt(eye, value).astype(jnp.bfloat16)

    def deal_copies(label, stream, i, buf, shift):
        return [
            remote(
                send.at[buf, shift + ring[d], :, span(i)],
                rows_in.at[stream, label, col, :, span(i)],
                a_send.at[label, stream, i, 0, d], a_recv.at[label, stream, i, d],
                {"expert": my_base + ring[d]},
            )
            for d in range(1, plane)
        ]

    def deal_across(label, stream, i, buf):
        return [
            remote(
                send.at[buf, plane + ring[d], :, span(i)],
                rows_in.at[stream, label, col, :, span(i)],
                a_send.at[label, stream, i, 1, d], a_recv.at[label, stream, i, d],
                {"expert": outer_base + ring[d]},
            )
            for d in range(plane)
        ]

    def deal(label, stream, i, source, buf, shift, amount):
        pick = picks[label, : amount * capacity]

        @pl.loop(i * part // STEP, (i + 1) * part // STEP)
        def _(k):
            cols = pl.ds(pl.multiple_of(k * STEP, STEP), STEP)
            rows = dot(pick, source[:, cols])
            send[buf, shift : shift + amount, :, cols] = rows.reshape(
                amount, capacity, STEP
            ).astype(jnp.bfloat16)

        start(deal_copies(label, stream, i, buf, shift))
        if amount == 2 * plane:
            start(deal_across(label, stream, i, buf))
        rows_in[stream, label, col, :, span(i)] = send[buf, shift + col, :, span(i)]

    def dealt(label, stream, i):
        source = send.at[0, 0, :, span(i)]
        target = rows_in.at[stream, label, 0, :, span(i)]

        def copy(d):
            return remote(
                source, target, a_send.at[label, stream, i, 0, d], a_recv.at[label, stream, i, d],
                near_inner,
            )

        arrived([copy(d) for d in range(1, plane)])
        if label != O:

            @pl.when(outer)
            def _():
                copy(0).wait_recv()

    def rows_of(buffer, cols):
        value = buffer[..., cols].astype(jnp.float32)
        return value.reshape(-1, value.shape[-1]).astype(jnp.bfloat16)

    def front_in(labels, i):
        count = len(labels) * block
        if i == 0:
            acc[0, :, :count] = jnp.zeros((2, count, acc.shape[3]), jnp.float32)
            acc[1, :, :count] = jnp.zeros((2, count, acc.shape[3]), jnp.float32)

        @pl.loop(i * part // STEP, (i + 1) * part // STEP)
        def _(k):
            cols = pl.ds(pl.multiple_of(k * STEP, STEP), STEP)
            rows = rows_of(rows_in.at[0, labels[0] : labels[-1] + 1], cols)
            for j in range(2):
                acc[0, j, :count] += dot(rows, gate_w[j, cols, :])
                acc[1, j, :count] += dot(rows, up_w[j, cols, :])

    def front_out(labels, i):
        count = len(labels) * block
        if i == 0:
            acc[2, :, :count] = jnp.zeros((2, count, acc.shape[3]), jnp.float32)

        @pl.loop(i * part // STEP, (i + 1) * part // STEP)
        def _(k):
            cols = pl.ds(pl.multiple_of(k * STEP, STEP), STEP)
            rows = rows_of(rows_in.at[1, labels[0] : labels[-1] + 1], cols)
            for j in range(2):
                acc[2, j, :count] += dot_nt(rows, down_w[j, :, cols])

    def pointwise(labels):
        count = len(labels) * block
        prob = jnp.zeros((count, 1), jnp.float32)
        for j in range(2):
            gating, lifted, grad_hidden = (acc[a, j, :count] for a in range(3))
            sigmoid = jax.nn.sigmoid(gating)
            active = gating * sigmoid
            hidden = (active * lifted).astype(jnp.bfloat16)
            prob += jnp.sum(hidden.astype(jnp.float32) * grad_hidden, axis=1, keepdims=True)
            slope_term = sigmoid * (1.0 + gating * (1.0 - sigmoid))
            grad_hid[0, j, :count] = (grad_hidden * lifted * slope_term).astype(jnp.bfloat16)
            grad_hid[1, j, :count] = (grad_hidden * active).astype(jnp.bfloat16)
        wide = jnp.broadcast_to(prob, (count, LANES)).reshape(-1, plane, capacity, LANES)
        rows_in[0, labels[0] : labels[-1] + 1, :, :, width:] = wide.astype(jnp.bfloat16)

    def slab(c):
        return pl.ds(c * piece, piece + (full - width if c == PIECES - 1 else 0))

    def home_copies(label, c):
        return [
            remote(
                rows_in.at[0, label, ring[d], :, slab(c)], back_in.at[label, col, :, slab(c)],
                b_send.at[label, c, 0, d], b_recv.at[label, c, 0, d],
                {"expert": my_base + ring[d]},
            )
            for d in range(1, plane)
        ]

    def home_across(label, c):
        return [
            remote(
                rows_in.at[0, label, ring[d], :, slab(c)],
                back_in.at[label, plane + col, :, slab(c)],
                b_send.at[label, c, 1, d], b_recv.at[label, c, 1, d],
                {"expert": inner_base + ring[d]},
            )
            for d in range(plane)
        ]

    def home(labels, c):
        count = len(labels) * block

        @pl.loop(c * piece // STEP, (c + 1) * piece // STEP)
        def _(k):
            cols = pl.ds(pl.multiple_of(k * STEP, STEP), STEP)
            total = dot_nt(grad_hid[0, 0, :count], gate_w[0, cols, :])
            total += dot_nt(grad_hid[0, 1, :count], gate_w[1, cols, :])
            total += dot_nt(grad_hid[1, 0, :count], up_w[0, cols, :])
            total += dot_nt(grad_hid[1, 1, :count], up_w[1, cols, :])
            rows_in[0, labels[0] : labels[-1] + 1, :, :, cols] = total.reshape(
                len(labels), plane, capacity, STEP
            ).astype(jnp.bfloat16)

        for label in labels:

            def within(label=label):
                start(home_copies(label, c))
                back_in[label, col, :, slab(c)] = rows_in[0, label, col, :, slab(c)]

            if label == O:
                within()
            else:
                pl.when(inner)(within)

                @pl.when(outer)
                def _():
                    start(home_across(label, c))

    def homed(label, c):
        arrived(home_copies(label, c))
        if label != O:
            arrived(home_across(label, c))

    def combine(label, c, amount, extra, target, values):
        count = amount * capacity

        @pl.loop(c * piece // STEP, (c + 1) * piece // STEP)
        def _(k):
            cols = pl.ds(pl.multiple_of(k * STEP, STEP), STEP)
            rows = rows_of(back_in.at[label, :amount], cols)
            total = dot(mats[label, 0, :, :count], rows) + dot(mats[label, 1, :, :count], rows)
            if extra is not None:
                total += extra[:, cols].astype(jnp.float32)
            target[:, cols] = total.astype(jnp.bfloat16)

        if c == PIECES - 1:
            rows = rows_of(back_in.at[label, :amount], pl.ds(width, LANES))
            lane = lax.broadcasted_iota(jnp.int32, (LANES, LANES), 1)
            total = jnp.where(
                lane < LANES // 2,
                dot(mats[label, 2, :, :count], rows),
                dot(mats[label, 3, :, :count], rows),
            )
            if extra is not None:
                total += extra[:, width:].astype(jnp.float32)
            values[...] = total.astype(jnp.bfloat16)

    def partial(which, c):
        return remote(
            land.at[1 + which, 0, :, slab(c)], part_in.at[which, :, slab(c)],
            p_send.at[which, c], p_recv.at[which, c], far_inner,
        )

    def last_hop(c):
        return remote(
            land.at[0, 0, :, slab(c)], land.at[0, 0, :, slab(c)], p_send.at[2, c], p_recv.at[2, c],
            near_outer,
        )

    def value_columns(ref):
        return ref.at[:, width:]

    parts, pieces, streams = range(PARTS), range(PIECES), range(2)

    @pl.when(inner)
    def _():
        tables(I, table[...], inner_base, outer_base, 2 * plane)

    @pl.when(outer)
    def _():
        tables(O, table[...], my_base, my_base, plane)

    for stream in streams:
        blocks[stream].wait()

        @pl.when(inner)
        def _():
            for i in parts:
                deal(I, stream, i, own.at[stream], stream, 0, 2 * plane)

        @pl.when(outer)
        def _():
            for i in parts:
                deal(O, stream, i, own.at[stream], stream, 0, plane)

    def pass_on(stream):
        for i in parts:
            up_block(stream, i, 0, near_inner).wait_recv()
            pass_block(stream, i).start()
            deal(O, stream, i, land.at[0, stream], 4, stream * plane, plane)

    def deal_far(label, target, stream, buf):
        for i in parts:
            up_block(stream, i, target, far_inner).wait_recv()
            deal(label, stream, i, land.at[target, stream], buf, 0, 2 * plane)

    @pl.when(inner)
    def _():
        up_table(0, near_inner).wait_recv()
        pass_table().start()
        tables(O, far_table[0], my_base, my_base, plane)
        up_table(1, far_inner).wait_recv()
        tables(FI, far_table[1], inner_base, outer_base, 2 * plane)
        pass_on(0)
        deal_far(FI, 1, 0, 2)

    for copy in locals_:
        copy.wait()
    arrived(swaps)
    near = (I, O)
    for i in parts:
        for label in near:
            dealt(label, 0, i)
        front_in(near, i)

    @pl.when(inner)
    def _():
        pass_on(1)
        deal_far(FI, 1, 1, 3)
        up_table(2, far_inner).wait_recv()
        tables(FO, far_table[2], inner_base, outer_base, 2 * plane)

    for i in parts:
        for label in near:
            dealt(label, 1, i)
        front_out(near, i)
    pointwise(near)
    for c in pieces:
        home(near, c)

    for i in parts:
        dealt(FI, 0, i)
        front_in((FI,), i)
    for i in parts:
        dealt(FI, 1, i)
        front_out((FI,), i)
    pointwise((FI,))
    for c in pieces:
        home((FI,), c)

    @pl.when(inner)
    def _():
        for stream in streams:
            for i in parts:
                sent(deal_copies(I, stream, i, stream, 0) + deal_across(I, stream, i, stream))
        deal_far(FO, 2, 0, 0)

    for i in parts:
        dealt(FO, 0, i)
        front_in((FO,), i)

    @pl.when(inner)
    def _():
        deal_far(FO, 2, 1, 1)
        for c in pieces:
            homed(FI, c)
            combine(FI, c, 2 * plane, None, land.at[1, 0], value_columns(land.at[1, 0]))
            partial(0, c).start()

    for i in parts:
        dealt(FO, 1, i)
        front_out((FO,), i)
    pointwise((FO,))
    for c in pieces:
        home((FO,), c)

    @pl.when(inner)
    def _():
        for c in pieces:
            homed(FO, c)
            combine(FO, c, 2 * plane, None, land.at[2, 0], value_columns(land.at[2, 0]))
            partial(1, c).start()
        for i in parts:
            pass_block(0, i).wait_send()
        for c in pieces:
            homed(I, c)
            partial(0, c).wait_recv()
            combine(I, c, 2 * plane, part_in.at[0], out, probs_out)
        for c in pieces:
            homed(O, c)
            partial(1, c).wait_recv()
            combine(O, c, plane, part_in.at[1], land.at[0, 0], value_columns(land.at[0, 0]))
            last_hop(c).start()
        sent(ups(1, far_inner) + [pass_table()])
        sent([pass_block(1, i) for i in parts])
        for stream in streams:
            for i in parts:
                sent(deal_copies(O, stream, i, 4, stream * plane))
                for label, buf in ((FI, 2), (FO, 0)):
                    sent(deal_copies(label, stream, i, buf + stream, 0))
                    sent(deal_across(label, stream, i, buf + stream))
        for c in pieces:
            for label in (I, FI, FO):
                sent(home_copies(label, c))
            sent([partial(0, c), partial(1, c), last_hop(c)])

    @pl.when(outer)
    def _():
        for c in pieces:
            homed(O, c)
            last_hop(c).wait_recv()
            combine(O, c, plane, land.at[0, 0], out, probs_out)
        sent(ups(0, near_inner))
        for stream in streams:
            for i in parts:
                sent(deal_copies(O, stream, i, stream, 0))
        for c in pieces:
            for label in (I, FI, FO):
                sent(home_across(label, c))

    for c in pieces:
        sent(home_copies(O, c))
    sent(swaps)


def fused_on_device(tokens, routes, route_probs, gate_weight, up_weight, down_weight, grad_out):
    tok_count, width = tokens.shape
    top_count = routes.shape[1]
    experts = lax.axis_size("expert")
    capacity = 3 * tok_count * top_count // (2 * experts)
    plane = experts // LAYERS
    hid = gate_weight.shape[2]
    full = width + LANES
    bf16, f32 = jnp.bfloat16, jnp.float32
    table = jnp.concatenate([routes.T.astype(f32), route_probs.T, jnp.zeros((4, tok_count), f32)])
    vmem, sems = pltpu.VMEM, pltpu.SemaphoreType.DMA
    spec = pl.BlockSpec(memory_space=pltpu.VMEM)
    raw = pl.BlockSpec(memory_space=pl.ANY)
    grad_tokens, values = pl.pallas_call(
        lambda *refs: fused_kernel(plane, *refs),
        name="routed_backward",
        out_shape=(
            jax.ShapeDtypeStruct((tok_count, width), bf16),
            jax.ShapeDtypeStruct((tok_count, LANES), bf16),
        ),
        in_specs=[spec] + [raw] * 5,
        out_specs=(spec, spec),
        scratch_shapes=[
            vmem((2, tok_count, width), bf16),
            vmem((4, 2 * plane * capacity, tok_count), bf16),
            vmem((4, 4, tok_count, 2 * plane * capacity), bf16),
            vmem((3, 8, tok_count), f32),
            vmem((3, 2, tok_count, full), bf16),
            vmem((2, width, hid), bf16),
            vmem((2, width, hid), bf16),
            vmem((2, hid, width), bf16),
            vmem((5, 2 * plane, capacity, width), bf16),
            vmem((2, 4, plane, capacity, full), bf16),
            vmem((3, 2, 2 * plane * capacity, hid), f32),
            vmem((2, 2, 2 * plane * capacity, hid), bf16),
            vmem((4, 2 * plane, capacity, full), bf16),
            vmem((2, tok_count, full), bf16),
            sems((5,)),
            sems((3,)), sems((3,)),
            sems((2,)), sems((3,)),
            sems((2, 2, PARTS)), sems((3, 2, PARTS)),
            sems((4, 2, PARTS, 2, plane)), sems((4, 2, PARTS, plane)),
            sems((4, PIECES, 2, plane)), sems((4, PIECES, 2, plane)),
            sems((3, PIECES)), sems((3, PIECES)),
        ],
        compiler_params=pltpu.CompilerParams(
            collective_id=0, has_side_effects=True, vmem_limit_bytes=63 * 1024 * 1024
        ),
    )(table, tokens, grad_out, gate_weight, up_weight, down_weight)
    return grad_tokens, values[:, :: LANES // 2]


def on_device(tokens, routes, *rest):
    experts = lax.axis_size("expert")
    capacity = 3 * routes.shape[0] * routes.shape[1] // (2 * experts)
    fits = capacity % 8 == 0 and lax.axis_size("seq") == 2 and routes.shape[1] == 2
    fits = fits and experts == LAYERS * (experts // LAYERS) and routes.shape[0] == LANES
    run = fused_on_device if fits else halves_on_device
    return run(tokens, routes, *rest)


def solution(mesh):
    placed = (
        P(("seq", "expert"), None),
        P(("seq", "expert"), None),
        P(("seq", "expert"), None),
        P("expert", None, "seq"),
        P("expert", None, "seq"),
        P("expert", "seq", None),
        P(("seq", "expert"), None),
    )
    return jax.shard_map(
        on_device,
        mesh=mesh,
        in_specs=placed,
        out_specs=(P(("seq", "expert"), None), P(("seq", "expert"), None)),
        check_vma=False,
    )
```

```python
import jax
import jax.numpy as jnp
from jax import lax
from jax.experimental import pallas as pl
from jax.experimental.pallas import tpu as pltpu
from jax.sharding import PartitionSpec as P

CHUNKS = 2
PIECES = 4
PARTS = 2
LAYERS = 4
LANES = 128
I, O, FI, FO = range(4)
RELAY = (I, FI, FO,)
STEP = 512
MESH = pl.DeviceIdType.MESH
NT = (((1,), (1,)), ((), ()))


def dot(a, b):
    return jnp.dot(a, b, preferred_element_type=jnp.float32)


def dot_nt(a, b):
    return lax.dot_general(a, b, NT, preferred_element_type=jnp.float32)


def slots_of(routes, base, half, capacity):
    local = routes - base
    chosen = local.reshape(-1)
    order = jnp.arange(chosen.shape[0], dtype=jnp.int32)
    earlier = (chosen[:, None] == chosen[None, :]) & (order[None, :] < order[:, None])
    position = jnp.sum(earlier.astype(jnp.int32), axis=1).reshape(routes.shape)
    valid = (local >= 0) & (local < half)
    return jnp.where(valid, local * capacity + position, -1)


def dispatch_of(slots, count):
    lanes = jnp.arange(count, dtype=jnp.int32)[:, None, None]
    return jnp.any(lanes == slots[None], axis=2).astype(jnp.bfloat16)


def weighting_of(slots, probs, count):
    lanes = jnp.arange(count, dtype=jnp.int32)[None, None, :]
    full = jnp.sum(jnp.where(slots[:, :, None] == lanes, probs[:, :, None], 0.0), axis=1)
    high = lax.reduce_precision(full, 8, 7)
    return high.astype(jnp.bfloat16), (full - high).astype(jnp.bfloat16)


def combine(weighting, rows):
    return dot(weighting[0], rows) + dot(weighting[1], rows)


def pick(slots, values):
    lanes = jnp.arange(values.shape[0], dtype=jnp.int32)[None, None, :]
    return jnp.sum(jnp.where(slots[:, :, None] == lanes, values[None, None, :], 0.0), axis=2)


def front(rows_in, gates, ups):
    return [(dot(rows_in, g), dot(rows_in, u)) for g, u in zip(gates, ups)]


def middle(terms, rows_grad, downs):
    prob, grads = 0.0, []
    for (gating, lifted), d in zip(terms, downs):
        sigmoid = jax.nn.sigmoid(gating)
        active = gating * sigmoid
        hidden = (active * lifted).astype(jnp.bfloat16)
        grad_hidden = dot_nt(rows_grad, d)
        prob = prob + jnp.sum(hidden.astype(jnp.float32) * grad_hidden, axis=1)
        slope_term = sigmoid * (1.0 + gating * (1.0 - sigmoid))
        grads.append(
            (
                (grad_hidden * lifted * slope_term).astype(jnp.bfloat16),
                (grad_hidden * active).astype(jnp.bfloat16),
            )
        )
    return grads, prob


def back(grads, gates, ups, columns):
    total = 0.0
    for (gg, gu), g, u in zip(grads, gates, ups):
        total = total + dot_nt(gg, g[columns]) + dot_nt(gu, u[columns])
    return total.astype(jnp.bfloat16)


def halves_on_device(tokens, routes, route_probs, gate_weight, up_weight, down_weight, grad_out):
    tok_count, width = tokens.shape
    top_count = routes.shape[1]
    experts = lax.axis_size("expert")
    parts = lax.axis_size("seq")
    capacity = 3 * tok_count * top_count // (2 * experts)
    half = experts // 2
    count = half * capacity
    base = (lax.axis_index("expert") // half) * half
    swap = [(i, (i + half) % experts) for i in range(experts)]
    groups = [list(range(half)), list(range(half, experts))]

    def across(value):
        return lax.ppermute(value, "expert", swap)

    def exchange(value):
        value = value.reshape(half, capacity, -1)
        value = lax.all_to_all(
            value, "expert", split_axis=0, concat_axis=0, tiled=True, axis_index_groups=groups
        )
        return value.reshape(count, -1)

    far_routes, far_probs = across(routes), across(route_probs)
    far_tokens, far_grad = across(tokens), across(grad_out)

    gates, ups, downs = [gate_weight[0]], [up_weight[0]], [down_weight[0]]
    for shift in range(1, parts):
        turn = [(i, (i + shift) % parts) for i in range(parts)]
        gates.append(lax.ppermute(gate_weight[0], "seq", turn))
        ups.append(lax.ppermute(up_weight[0], "seq", turn))
        downs.append(lax.ppermute(down_weight[0], "seq", turn))

    near_slots = slots_of(routes, base, half, capacity)
    near_pick = dispatch_of(near_slots, count)
    near_in = exchange(dot(near_pick, tokens).astype(jnp.bfloat16))
    near_out = exchange(dot(near_pick, grad_out).astype(jnp.bfloat16))
    near_grads, near_prob = middle(front(near_in, gates, ups), near_out, downs)

    far_slots = slots_of(far_routes, base, half, capacity)
    far_pick = dispatch_of(far_slots, count)
    far_in = exchange(dot(far_pick, far_tokens).astype(jnp.bfloat16))
    far_terms = front(far_in, gates, ups)
    far_out = exchange(dot(far_pick, far_grad).astype(jnp.bfloat16))
    far_grads, far_prob = middle(far_terms, far_out, downs)

    near_weighting = weighting_of(near_slots, route_probs, count)
    far_weighting = weighting_of(far_slots, far_probs, count)

    size = width // CHUNKS
    spans = [slice(c * size, (c + 1) * size) for c in range(CHUNKS)]

    def send_back(grads, prob, span):
        rows = back(grads, gates, ups, span)
        if span.start == 0:
            column = jnp.broadcast_to(prob.astype(jnp.bfloat16)[:, None], (count, 128))
            rows = jnp.concatenate([rows, column], axis=1)
        return exchange(rows)

    returned = []
    for span in spans:
        rows = send_back(far_grads, far_prob, span)
        partial = combine(far_weighting, rows[:, :size]).astype(jnp.bfloat16)
        returned.append(across(partial))
        if span.start == 0:
            far_values = pick(far_slots, rows[:, size].astype(jnp.float32))
            far_values = across(far_values.astype(jnp.bfloat16))
    pieces = []
    for span, far_piece in zip(spans, returned):
        rows = send_back(near_grads, near_prob, span)
        near_piece = combine(near_weighting, rows[:, :size])
        pieces.append((near_piece + far_piece.astype(jnp.float32)).astype(jnp.bfloat16))
        if span.start == 0:
            near_values = pick(near_slots, rows[:, size].astype(jnp.float32))
    grad_probs = (near_values + far_values.astype(jnp.float32)).astype(jnp.bfloat16)
    return (jnp.concatenate(pieces, axis=1), grad_probs)


def fused_kernel(
    plane,
    table, tok_hbm, grad_hbm, gate_hbm, up_hbm, down_hbm,
    out, probs_out,
    own, picks, mats, far_table, land, gate_w, up_w, down_w, send, rows_in, acc, grad_hid, back_in,
    part_in,
    local_sem, w_send, w_recv, t_send, t_recv, x_send, x_recv, a_send, a_recv, b_send, b_recv,
    p_send, p_recv,
):
    width, capacity = own.shape[2], send.shape[2]
    full = land.shape[3]
    block = plane * capacity
    piece, part = width // PIECES, width // PARTS
    me = lax.axis_index("expert")
    core = lax.axis_index("seq")
    layer = me // plane
    col = me - layer * plane
    side = layer // (LAYERS // 2)
    inner = (layer == 1) | (layer == 2)
    outer = jnp.logical_not(inner)
    my_base, inner_base = layer * plane, (side + 1) * plane
    outer_base = side * (LAYERS - 1) * plane
    twin = {"seq": 1 - core}
    near_inner = {"expert": inner_base + col}
    near_outer = {"expert": outer_base + col}
    far_inner = {"expert": (2 - side) * plane + col}
    ring = [lax.rem(col + d, plane) for d in range(plane)]

    def remote(src, dst, ss, rs, device):
        return pltpu.make_async_remote_copy(
            src_ref=src, dst_ref=dst, send_sem=ss, recv_sem=rs,
            device_id=device, device_id_type=MESH,
        )

    def start(copies):
        for copy in copies:
            copy.start()

    def arrived(copies):
        for copy in copies:
            copy.wait_recv()

    def sent(copies):
        for copy in copies:
            copy.wait_send()

    weights = ((gate_hbm, gate_w), (up_hbm, up_w), (down_hbm, down_w))
    blocks = [
        pltpu.make_async_copy(src, own.at[i], local_sem.at[i])
        for i, src in enumerate((tok_hbm, grad_hbm))
    ]
    locals_ = [
        pltpu.make_async_copy(src.at[0], dst.at[0], local_sem.at[2 + i])
        for i, (src, dst) in enumerate(weights)
    ]
    start(blocks + locals_)

    barrier = pltpu.get_barrier_semaphore()

    def greet(device):
        pl.semaphore_signal(barrier, inc=1, device_id=device, device_id_type=MESH)

    greet(twin)
    for d in range(1, plane):
        greet({"expert": my_base + ring[d]})

    @pl.when(inner)
    def _():
        greet(far_inner)
        for d in range(plane):
            greet({"expert": outer_base + ring[d]})
        pl.semaphore_wait(barrier, 2 * plane + 1)

    @pl.when(outer)
    def _():
        for d in range(plane):
            greet({"expert": inner_base + ring[d]})
        pl.semaphore_wait(barrier, 2 * plane)

    def span(i):
        return pl.ds(i * part, part)

    def up_table(target, device):
        return remote(table, far_table.at[target], t_send.at[0], t_recv.at[target], device)

    def up_block(stream, i, target, device):
        source = (tok_hbm, grad_hbm)[stream]
        return remote(
            source.at[:, span(i)], land.at[target, stream, :, span(i)],
            x_send.at[0, stream, i], x_recv.at[target, stream, i], device,
        )

    def pass_table():
        return remote(far_table.at[0], far_table.at[2], t_send.at[1], t_recv.at[2], far_inner)

    def pass_block(stream, i):
        return remote(
            land.at[0, stream, :, span(i)], land.at[2, stream, :, span(i)],
            x_send.at[1, stream, i], x_recv.at[2, stream, i], far_inner,
        )

    def ups(target, device, streams=(0, 1)):
        return [up_block(stream, i, target, device) for stream in streams for i in range(PARTS)]

    @pl.when(inner)
    def _():
        start([up_table(1, far_inner)] + ups(1, far_inner, (0,)))

    @pl.when(outer)
    def _():
        start([up_table(0, near_inner)] + ups(0, near_inner))

    swaps = [
        remote(src.at[0], dst.at[1], w_send.at[i], w_recv.at[i], twin)
        for i, (src, dst) in enumerate(weights)
    ]
    start(swaps)

    def tables(label, values, first, second, amount):
        count = amount * capacity
        p = lax.broadcasted_iota(jnp.int32, (amount, LANES), 0)
        expert = jnp.where(p < plane, first + p, second + p - plane).astype(jnp.float32)
        named = [jnp.where(values[k : k + 1] == expert, 1.0, 0.0) for k in range(2)]
        before = lax.broadcasted_iota(jnp.int32, (LANES, LANES), 0)
        after = lax.broadcasted_iota(jnp.int32, (LANES, LANES), 1)
        lower = jnp.where(before < after, 1.0, 0.0).astype(jnp.bfloat16)
        eye = jnp.where(before == after, 1.0, 0.0).astype(jnp.bfloat16)
        position = dot((named[0] + named[1]).astype(jnp.bfloat16), lower)
        place = lax.broadcasted_iota(jnp.int32, (amount, capacity, LANES), 1).astype(jnp.float32)
        hit = jnp.where(position[:, None, :] == place, 1.0, 0.0)
        chosen = [(hit * n[:, None, :]).reshape(count, LANES) for n in named]
        picks[label, :count] = (chosen[0] + chosen[1]).astype(jnp.bfloat16)
        weight = chosen[0] * values[2:3] + chosen[1] * values[3:4]
        high = weight.astype(jnp.bfloat16)
        low = (weight - high.astype(jnp.float32)).astype(jnp.bfloat16)
        for i, value in enumerate((high, low, *(c.astype(jnp.bfloat16) for c in chosen))):
            mats[label, i, :, :count] = dot_nt(eye, value).astype(jnp.bfloat16)

    def deal_copies(label, stream, i, buf, shift):
        return [
            remote(
                send.at[buf, shift + ring[d], :, span(i)],
                rows_in.at[stream, label, col, :, span(i)],
                a_send.at[label, stream, i, 0, d], a_recv.at[label, stream, i, d],
                {"expert": my_base + ring[d]},
            )
            for d in range(1, plane)
        ]

    def deal_across(label, stream, i, buf):
        return [
            remote(
                send.at[buf, plane + ring[d], :, span(i)],
                rows_in.at[stream, label, col, :, span(i)],
                a_send.at[label, stream, i, 1, d], a_recv.at[label, stream, i, d],
                {"expert": outer_base + ring[d]},
            )
            for d in range(plane)
        ]

    def deal(label, stream, i, source, buf, shift, amount):
        pick = picks[label, : amount * capacity]

        @pl.loop(i * part // STEP, (i + 1) * part // STEP)
        def _(k):
            cols = pl.ds(pl.multiple_of(k * STEP, STEP), STEP)
            rows = dot(pick, source[:, cols])
            send[buf, shift : shift + amount, :, cols] = rows.reshape(
                amount, capacity, STEP
            ).astype(jnp.bfloat16)

        start(deal_copies(label, stream, i, buf, shift))
        if amount == 2 * plane:
            start(deal_across(label, stream, i, buf))
        rows_in[stream, label, col, :, span(i)] = send[buf, shift + col, :, span(i)]

    def dealt(label, stream, i):
        source = send.at[0, 0, :, span(i)]
        target = rows_in.at[stream, label, 0, :, span(i)]

        def copy(d):
            return remote(
                source, target, a_send.at[label, stream, i, 0, d], a_recv.at[label, stream, i, d],
                near_inner,
            )

        arrived([copy(d) for d in range(1, plane)])
        if label != O:

            @pl.when(outer)
            def _():
                copy(0).wait_recv()

    def rows_of(buffer, cols):
        value = buffer[..., cols].astype(jnp.float32)
        return value.reshape(-1, value.shape[-1]).astype(jnp.bfloat16)

    def sums_for(labels):
        first = min(labels[0], FI) * block
        return slice(first, first + len(labels) * block)

    def front_in(labels, i):
        count, sums = len(labels) * block, sums_for(labels)
        if i == 0:
            acc[0, :, sums] = jnp.zeros((2, count, acc.shape[3]), jnp.float32)
            acc[1, :, sums] = jnp.zeros((2, count, acc.shape[3]), jnp.float32)

        @pl.loop(i * part // STEP, (i + 1) * part // STEP)
        def _(k):
            cols = pl.ds(pl.multiple_of(k * STEP, STEP), STEP)
            rows = rows_of(rows_in.at[0, labels[0] : labels[-1] + 1], cols)
            for j in range(2):
                acc[0, j, sums] += dot(rows, gate_w[j, cols, :])
                acc[1, j, sums] += dot(rows, up_w[j, cols, :])

    def front_out(labels, i):
        count, sums = len(labels) * block, sums_for(labels)
        if i == 0:
            acc[2, :, sums] = jnp.zeros((2, count, acc.shape[3]), jnp.float32)

        @pl.loop(i * part // STEP, (i + 1) * part // STEP)
        def _(k):
            cols = pl.ds(pl.multiple_of(k * STEP, STEP), STEP)
            rows = rows_of(rows_in.at[1, labels[0] : labels[-1] + 1], cols)
            for j in range(2):
                acc[2, j, sums] += dot_nt(rows, down_w[j, :, cols])

    def rows_for(labels):
        return slice(labels[0] * block, (labels[-1] + 1) * block)

    def pointwise(labels):
        count, rows = len(labels) * block, rows_for(labels)
        prob = jnp.zeros((count, 1), jnp.float32)
        for j in range(2):
            gating, lifted, grad_hidden = (acc[a, j, sums_for(labels)] for a in range(3))
            sigmoid = jax.nn.sigmoid(gating)
            active = gating * sigmoid
            hidden = (active * lifted).astype(jnp.bfloat16)
            prob += jnp.sum(hidden.astype(jnp.float32) * grad_hidden, axis=1, keepdims=True)
            slope_term = sigmoid * (1.0 + gating * (1.0 - sigmoid))
            grad_hid[0, j, rows] = (grad_hidden * lifted * slope_term).astype(jnp.bfloat16)
            grad_hid[1, j, rows] = (grad_hidden * active).astype(jnp.bfloat16)
        wide = jnp.broadcast_to(prob, (count, LANES)).reshape(-1, plane, capacity, LANES)
        rows_in[0, labels[0] : labels[-1] + 1, :, :, width:] = wide.astype(jnp.bfloat16)

    def slab(c):
        return pl.ds(c * piece, piece + (full - width if c == PIECES - 1 else 0))

    def home_copies(label, c):
        return [
            remote(
                rows_in.at[0, label, ring[d], :, slab(c)], back_in.at[label, col, :, slab(c)],
                b_send.at[label, c, 0, d], b_recv.at[label, c, 0, d],
                {"expert": my_base + ring[d]},
            )
            for d in range(1, plane)
        ]

    def home_across(label, c):
        return [
            remote(
                rows_in.at[0, label, ring[d], :, slab(c)],
                back_in.at[label, plane + col, :, slab(c)],
                b_send.at[label, c, 1, d], b_recv.at[label, c, 1, d],
                {"expert": inner_base + ring[d]},
            )
            for d in range(plane)
        ]

    def home(labels, c):
        rows = rows_for(labels)

        @pl.loop(c * piece // STEP, (c + 1) * piece // STEP)
        def _(k):
            cols = pl.ds(pl.multiple_of(k * STEP, STEP), STEP)
            total = dot_nt(grad_hid[0, 0, rows], gate_w[0, cols, :])
            total += dot_nt(grad_hid[0, 1, rows], gate_w[1, cols, :])
            total += dot_nt(grad_hid[1, 0, rows], up_w[0, cols, :])
            total += dot_nt(grad_hid[1, 1, rows], up_w[1, cols, :])
            rows_in[0, labels[0] : labels[-1] + 1, :, :, cols] = total.reshape(
                len(labels), plane, capacity, STEP
            ).astype(jnp.bfloat16)

    def go_home(labels, c):
        for label in labels:

            def within(label=label):
                start(home_copies(label, c))
                back_in[label, col, :, slab(c)] = rows_in[0, label, col, :, slab(c)]

            if label == O or label in RELAY:
                within()
            else:
                pl.when(inner)(within)

                @pl.when(outer)
                def _():
                    start(home_across(label, c))

    def relay_copy(label, c):
        return remote(
            back_in.at[label, :plane, :, slab(c)], back_in.at[label, plane:, :, slab(c)],
            b_send.at[label, c, 1, 0], b_recv.at[label, c, 1, 0], near_inner,
        )

    def relay(label):
        @pl.when(outer)
        def _():
            for c in pieces:
                arrived(home_copies(label, c))
                relay_copy(label, c).start()

    def homed(label, c):
        arrived(home_copies(label, c))
        if label in RELAY:
            relay_copy(label, c).wait_recv()
        elif label != O:
            arrived(home_across(label, c))

    def combine(label, c, amount, extra, target, values):
        count = amount * capacity

        @pl.loop(c * piece // STEP, (c + 1) * piece // STEP)
        def _(k):
            cols = pl.ds(pl.multiple_of(k * STEP, STEP), STEP)
            rows = rows_of(back_in.at[label, :amount], cols)
            total = dot(mats[label, 0, :, :count], rows) + dot(mats[label, 1, :, :count], rows)
            if extra is not None:
                total += extra[:, cols].astype(jnp.float32)
            target[:, cols] = total.astype(jnp.bfloat16)

        if c == PIECES - 1:
            rows = rows_of(back_in.at[label, :amount], pl.ds(width, LANES))
            lane = lax.broadcasted_iota(jnp.int32, (LANES, LANES), 1)
            total = jnp.where(
                lane < LANES // 2,
                dot(mats[label, 2, :, :count], rows),
                dot(mats[label, 3, :, :count], rows),
            )
            if extra is not None:
                total += extra[:, width:].astype(jnp.float32)
            values[...] = total.astype(jnp.bfloat16)

    def partial(which, c):
        return remote(
            land.at[1 + which, 0, :, slab(c)], part_in.at[which, :, slab(c)],
            p_send.at[which, c], p_recv.at[which, c], far_inner,
        )

    def last_hop(c):
        return remote(
            land.at[0, 0, :, slab(c)], land.at[0, 0, :, slab(c)], p_send.at[2, c], p_recv.at[2, c],
            near_outer,
        )

    def value_columns(ref):
        return ref.at[:, width:]

    parts, pieces, streams = range(PARTS), range(PIECES), range(2)

    @pl.when(inner)
    def _():
        tables(I, table[...], inner_base, outer_base, 2 * plane)

    @pl.when(outer)
    def _():
        tables(O, table[...], my_base, my_base, plane)

    for stream in streams:
        blocks[stream].wait()

        @pl.when(inner)
        def _():
            for i in parts:
                deal(I, stream, i, own.at[stream], stream, 0, 2 * plane)

        @pl.when(outer)
        def _():
            for i in parts:
                deal(O, stream, i, own.at[stream], stream, 0, plane)

    def own_sent():
        @pl.when(inner)
        def _():
            sent([up_table(1, far_inner)] + ups(1, far_inner))

    def cross_grads():
        @pl.when(inner)
        def _():
            start(ups(1, far_inner, (1,)))

    def pass_outer(stream):
        @pl.when(inner)
        def _():
            for i in parts:
                up_block(stream, i, 0, near_inner).wait_recv()
                pass_block(stream, i).start()
                deal(O, stream, i, land.at[0, stream], 4, stream * plane, plane)

    def deal_far(label, target, stream, buf):
        @pl.when(inner)
        def _():
            for i in parts:
                up_block(stream, i, target, far_inner).wait_recv()
                deal(label, stream, i, land.at[target, stream], buf, 0, 2 * plane)

    def outer_tables():
        @pl.when(inner)
        def _():
            up_table(0, near_inner).wait_recv()
            pass_table().start()
            tables(O, far_table[0], my_base, my_base, plane)

    def far_tables(label):
        @pl.when(inner)
        def _():
            up_table(label - 1, far_inner).wait_recv()
            tables(label, far_table[label - 1], inner_base, outer_base, 2 * plane)

    def own_dealt():
        @pl.when(inner)
        def _():
            for stream in streams:
                for i in parts:
                    sent(deal_copies(I, stream, i, stream, 0) + deal_across(I, stream, i, stream))

    near = (I, O)

    def take_weights():
        for copy in locals_:
            copy.wait()
        arrived(swaps)

    def front(labels):
        for i in parts:
            for label in labels:
                dealt(label, 0, i)
            front_in(labels, i)

    def finish(labels):
        for i in parts:
            for label in labels:
                dealt(label, 1, i)
            front_out(labels, i)
        pointwise(labels)

    def make_home(labels):
        for c in pieces:
            home(labels, c)

    def start_home(labels):
        for c in pieces:
            go_home(labels, c)

    def send_home(labels):
        for c in pieces:
            home(labels, c)
            go_home(labels, c)

    def cross_back(label, which):
        @pl.when(inner)
        def _():
            target = land.at[1 + which, 0]
            for c in pieces:
                homed(label, c)
                combine(label, c, 2 * plane, None, target, value_columns(target))
                partial(which, c).start()

    def own_result():
        @pl.when(inner)
        def _():
            for c in pieces:
                homed(I, c)
                partial(0, c).wait_recv()
                combine(I, c, 2 * plane, part_in.at[0], out, probs_out)

    def outer_result():
        @pl.when(inner)
        def _():
            for i in parts:
                pass_block(0, i).wait_send()
            for c in pieces:
                homed(O, c)
                partial(1, c).wait_recv()
                combine(O, c, plane, part_in.at[1], land.at[0, 0], value_columns(land.at[0, 0]))
                last_hop(c).start()

        @pl.when(outer)
        def _():
            for c in pieces:
                homed(O, c)
                last_hop(c).wait_recv()
                combine(O, c, plane, land.at[0, 0], out, probs_out)

    outer_tables()
    far_tables(FI)
    pass_outer(0)
    deal_far(FI, 1, 0, 2)
    take_weights()
    front(near)
    pass_outer(1)
    cross_grads()
    far_tables(FO)
    own_dealt()
    deal_far(FO, 2, 0, 0)
    finish(near)
    make_home(near)
    start_home((I,))
    front((FO,))
    deal_far(FO, 2, 1, 1)
    relay(I)
    finish((FO,))
    send_home((FO,))
    relay(FO)
    front((FI,))
    deal_far(FI, 1, 1, 3)
    cross_back(FO, 1)
    finish((FI,))
    send_home((FI,))
    relay(FI)
    start_home((O,))
    cross_back(FI, 0)
    outer_result()
    own_result()
    own_sent()

    @pl.when(inner)
    def _():
        pass_table().wait_send()
        sent([pass_block(1, i) for i in parts])
        for stream in streams:
            for i in parts:
                sent(deal_copies(O, stream, i, 4, stream * plane))
                for label, buf in ((FI, 2), (FO, 0)):
                    sent(deal_copies(label, stream, i, buf + stream, 0))
                    sent(deal_across(label, stream, i, buf + stream))
        for c in pieces:
            for label in (I, FI, FO):
                sent(home_copies(label, c))
            sent([partial(0, c), partial(1, c), last_hop(c)])

    @pl.when(outer)
    def _():
        sent([up_table(0, near_inner)] + ups(0, near_inner))
        for stream in streams:
            for i in parts:
                sent(deal_copies(O, stream, i, stream, 0))
        for c in pieces:
            for label in (I, FI, FO):
                if label in RELAY:
                    sent([*home_copies(label, c), relay_copy(label, c)])
                else:
                    sent(home_across(label, c))

    for c in pieces:
        sent(home_copies(O, c))
    sent(swaps)


def fused_on_device(tokens, routes, route_probs, gate_weight, up_weight, down_weight, grad_out):
    tok_count, width = tokens.shape
    top_count = routes.shape[1]
    experts = lax.axis_size("expert")
    capacity = 3 * tok_count * top_count // (2 * experts)
    plane = experts // LAYERS
    hid = gate_weight.shape[2]
    full = width + LANES
    bf16, f32 = jnp.bfloat16, jnp.float32
    table = jnp.concatenate([routes.T.astype(f32), route_probs.T, jnp.zeros((4, tok_count), f32)])
    vmem, sems = pltpu.VMEM, pltpu.SemaphoreType.DMA
    spec = pl.BlockSpec(memory_space=pltpu.VMEM)
    raw = pl.BlockSpec(memory_space=pl.ANY)
    grad_tokens, values = pl.pallas_call(
        lambda *refs: fused_kernel(plane, *refs),
        name="routed_backward",
        out_shape=(
            jax.ShapeDtypeStruct((tok_count, width), bf16),
            jax.ShapeDtypeStruct((tok_count, LANES), bf16),
        ),
        in_specs=[spec] + [raw] * 5,
        out_specs=(spec, spec),
        scratch_shapes=[
            vmem((2, tok_count, width), bf16),
            vmem((4, 2 * plane * capacity, tok_count), bf16),
            vmem((4, 4, tok_count, 2 * plane * capacity), bf16),
            vmem((3, 8, tok_count), f32),
            vmem((3, 2, tok_count, full), bf16),
            vmem((2, width, hid), bf16),
            vmem((2, width, hid), bf16),
            vmem((2, hid, width), bf16),
            vmem((5, 2 * plane, capacity, width), bf16),
            vmem((2, 4, plane, capacity, full), bf16),
            vmem((3, 2, 3 * plane * capacity, hid), f32),
            vmem((2, 2, 4 * plane * capacity, hid), bf16),
            vmem((4, 2 * plane, capacity, full), bf16),
            vmem((2, tok_count, full), bf16),
            sems((5,)),
            sems((3,)), sems((3,)),
            sems((2,)), sems((3,)),
            sems((2, 2, PARTS)), sems((3, 2, PARTS)),
            sems((4, 2, PARTS, 2, plane)), sems((4, 2, PARTS, plane)),
            sems((4, PIECES, 2, plane)), sems((4, PIECES, 2, plane)),
            sems((3, PIECES)), sems((3, PIECES)),
        ],
        compiler_params=pltpu.CompilerParams(
            collective_id=0, has_side_effects=True, vmem_limit_bytes=63 * 1024 * 1024
        ),
    )(table, tokens, grad_out, gate_weight, up_weight, down_weight)
    return grad_tokens, values[:, :: LANES // 2]


def on_device(tokens, routes, *rest):
    experts = lax.axis_size("expert")
    capacity = 3 * routes.shape[0] * routes.shape[1] // (2 * experts)
    fits = capacity % 8 == 0 and lax.axis_size("seq") == 2 and routes.shape[1] == 2
    fits = fits and experts == LAYERS * (experts // LAYERS) and routes.shape[0] == LANES
    run = fused_on_device if fits else halves_on_device
    return run(tokens, routes, *rest)


def solution(mesh):
    placed = (
        P(("seq", "expert"), None),
        P(("seq", "expert"), None),
        P(("seq", "expert"), None),
        P("expert", None, "seq"),
        P("expert", None, "seq"),
        P("expert", "seq", None),
        P(("seq", "expert"), None),
    )
    return jax.shard_map(
        on_device,
        mesh=mesh,
        in_specs=placed,
        out_specs=(P(("seq", "expert"), None), P(("seq", "expert"), None)),
        check_vma=False,
    )
```

```python
import jax
import jax.numpy as jnp
from jax import lax
from jax.experimental import pallas as pl
from jax.experimental.pallas import tpu as pltpu
from jax.sharding import PartitionSpec as P

CHUNKS = 2
PIECES = 4
PARTS = 2
LAYERS = 4
LANES = 128
I, O, FI, FO = range(4)
STEP = 512
MESH = pl.DeviceIdType.MESH
NT = (((1,), (1,)), ((), ()))


def dot(a, b):
    return jnp.dot(a, b, preferred_element_type=jnp.float32)


def dot_nt(a, b):
    return lax.dot_general(a, b, NT, preferred_element_type=jnp.float32)


def slots_of(routes, base, half, capacity):
    local = routes - base
    chosen = local.reshape(-1)
    order = jnp.arange(chosen.shape[0], dtype=jnp.int32)
    earlier = (chosen[:, None] == chosen[None, :]) & (order[None, :] < order[:, None])
    position = jnp.sum(earlier.astype(jnp.int32), axis=1).reshape(routes.shape)
    valid = (local >= 0) & (local < half)
    return jnp.where(valid, local * capacity + position, -1)


def dispatch_of(slots, count):
    lanes = jnp.arange(count, dtype=jnp.int32)[:, None, None]
    return jnp.any(lanes == slots[None], axis=2).astype(jnp.bfloat16)


def weighting_of(slots, probs, count):
    lanes = jnp.arange(count, dtype=jnp.int32)[None, None, :]
    full = jnp.sum(jnp.where(slots[:, :, None] == lanes, probs[:, :, None], 0.0), axis=1)
    high = lax.reduce_precision(full, 8, 7)
    return high.astype(jnp.bfloat16), (full - high).astype(jnp.bfloat16)


def combine(weighting, rows):
    return dot(weighting[0], rows) + dot(weighting[1], rows)


def pick(slots, values):
    lanes = jnp.arange(values.shape[0], dtype=jnp.int32)[None, None, :]
    return jnp.sum(jnp.where(slots[:, :, None] == lanes, values[None, None, :], 0.0), axis=2)


def front(rows_in, gates, ups):
    return [(dot(rows_in, g), dot(rows_in, u)) for g, u in zip(gates, ups)]


def middle(terms, rows_grad, downs):
    prob, grads = 0.0, []
    for (gating, lifted), d in zip(terms, downs):
        sigmoid = jax.nn.sigmoid(gating)
        active = gating * sigmoid
        hidden = (active * lifted).astype(jnp.bfloat16)
        grad_hidden = dot_nt(rows_grad, d)
        prob = prob + jnp.sum(hidden.astype(jnp.float32) * grad_hidden, axis=1)
        slope_term = sigmoid * (1.0 + gating * (1.0 - sigmoid))
        grads.append(
            (
                (grad_hidden * lifted * slope_term).astype(jnp.bfloat16),
                (grad_hidden * active).astype(jnp.bfloat16),
            )
        )
    return grads, prob


def back(grads, gates, ups, columns):
    total = 0.0
    for (gg, gu), g, u in zip(grads, gates, ups):
        total = total + dot_nt(gg, g[columns]) + dot_nt(gu, u[columns])
    return total.astype(jnp.bfloat16)


def halves_on_device(tokens, routes, route_probs, gate_weight, up_weight, down_weight, grad_out):
    tok_count, width = tokens.shape
    top_count = routes.shape[1]
    experts = lax.axis_size("expert")
    parts = lax.axis_size("seq")
    capacity = 3 * tok_count * top_count // (2 * experts)
    half = experts // 2
    count = half * capacity
    base = (lax.axis_index("expert") // half) * half
    swap = [(i, (i + half) % experts) for i in range(experts)]
    groups = [list(range(half)), list(range(half, experts))]

    def across(value):
        return lax.ppermute(value, "expert", swap)

    def exchange(value):
        value = value.reshape(half, capacity, -1)
        value = lax.all_to_all(
            value, "expert", split_axis=0, concat_axis=0, tiled=True, axis_index_groups=groups
        )
        return value.reshape(count, -1)

    far_routes, far_probs = across(routes), across(route_probs)
    far_tokens, far_grad = across(tokens), across(grad_out)

    gates, ups, downs = [gate_weight[0]], [up_weight[0]], [down_weight[0]]
    for shift in range(1, parts):
        turn = [(i, (i + shift) % parts) for i in range(parts)]
        gates.append(lax.ppermute(gate_weight[0], "seq", turn))
        ups.append(lax.ppermute(up_weight[0], "seq", turn))
        downs.append(lax.ppermute(down_weight[0], "seq", turn))

    near_slots = slots_of(routes, base, half, capacity)
    near_pick = dispatch_of(near_slots, count)
    near_in = exchange(dot(near_pick, tokens).astype(jnp.bfloat16))
    near_out = exchange(dot(near_pick, grad_out).astype(jnp.bfloat16))
    near_grads, near_prob = middle(front(near_in, gates, ups), near_out, downs)

    far_slots = slots_of(far_routes, base, half, capacity)
    far_pick = dispatch_of(far_slots, count)
    far_in = exchange(dot(far_pick, far_tokens).astype(jnp.bfloat16))
    far_terms = front(far_in, gates, ups)
    far_out = exchange(dot(far_pick, far_grad).astype(jnp.bfloat16))
    far_grads, far_prob = middle(far_terms, far_out, downs)

    near_weighting = weighting_of(near_slots, route_probs, count)
    far_weighting = weighting_of(far_slots, far_probs, count)

    size = width // CHUNKS
    spans = [slice(c * size, (c + 1) * size) for c in range(CHUNKS)]

    def send_back(grads, prob, span):
        rows = back(grads, gates, ups, span)
        if span.start == 0:
            column = jnp.broadcast_to(prob.astype(jnp.bfloat16)[:, None], (count, 128))
            rows = jnp.concatenate([rows, column], axis=1)
        return exchange(rows)

    returned = []
    for span in spans:
        rows = send_back(far_grads, far_prob, span)
        partial = combine(far_weighting, rows[:, :size]).astype(jnp.bfloat16)
        returned.append(across(partial))
        if span.start == 0:
            far_values = pick(far_slots, rows[:, size].astype(jnp.float32))
            far_values = across(far_values.astype(jnp.bfloat16))
    pieces = []
    for span, far_piece in zip(spans, returned):
        rows = send_back(near_grads, near_prob, span)
        near_piece = combine(near_weighting, rows[:, :size])
        pieces.append((near_piece + far_piece.astype(jnp.float32)).astype(jnp.bfloat16))
        if span.start == 0:
            near_values = pick(near_slots, rows[:, size].astype(jnp.float32))
    grad_probs = (near_values + far_values.astype(jnp.float32)).astype(jnp.bfloat16)
    return (jnp.concatenate(pieces, axis=1), grad_probs)


def fused_kernel(
    plane,
    routes, probs, tok_hbm, grad_hbm, gate_hbm, up_hbm, down_hbm,
    out, probs_out,
    table, own, picks, mats, far_table, land, gate_w, up_w, down_w, send, rows_in, acc, grad_hid, back_in,
    part_in,
    local_sem, w_send, w_recv, t_send, t_recv, x_send, x_recv, a_send, a_recv, b_send, b_recv,
    p_send, p_recv,
):
    width, capacity = own.shape[2], send.shape[2]
    full = land.shape[3]
    block = plane * capacity
    piece, part = width // PIECES, width // PARTS
    me = lax.axis_index("expert")
    core = lax.axis_index("seq")
    layer = me // plane
    col = me - layer * plane
    side = layer // (LAYERS // 2)
    inner = (layer == 1) | (layer == 2)
    outer = jnp.logical_not(inner)
    my_base, inner_base = layer * plane, (side + 1) * plane
    outer_base = side * (LAYERS - 1) * plane
    twin = {"seq": 1 - core}
    near_inner = {"expert": inner_base + col}
    near_outer = {"expert": outer_base + col}
    far_inner = {"expert": (2 - side) * plane + col}
    ring = [lax.rem(col + d, plane) for d in range(plane)]

    def remote(src, dst, ss, rs, device):
        return pltpu.make_async_remote_copy(
            src_ref=src, dst_ref=dst, send_sem=ss, recv_sem=rs,
            device_id=device, device_id_type=MESH,
        )

    def start(copies):
        for copy in copies:
            copy.start()

    def arrived(copies):
        for copy in copies:
            copy.wait_recv()

    def sent(copies):
        for copy in copies:
            copy.wait_send()

    weights = ((gate_hbm, gate_w), (up_hbm, up_w), (down_hbm, down_w))
    blocks = [
        pltpu.make_async_copy(src, own.at[i], local_sem.at[i])
        for i, src in enumerate((tok_hbm, grad_hbm))
    ]
    locals_ = [
        pltpu.make_async_copy(src.at[0], dst.at[0], local_sem.at[2 + i])
        for i, (src, dst) in enumerate(weights)
    ]
    start(blocks + locals_)

    table[:2] = routes[...].astype(jnp.float32)
    table[2:4] = probs[...]
    table[4:] = jnp.zeros((4, LANES), jnp.float32)
    barrier = pltpu.get_barrier_semaphore()

    def greet(device):
        pl.semaphore_signal(barrier, inc=1, device_id=device, device_id_type=MESH)

    greet(twin)
    for d in range(1, plane):
        greet({"expert": my_base + ring[d]})

    @pl.when(inner)
    def _():
        greet(far_inner)
        for d in range(plane):
            greet({"expert": outer_base + ring[d]})
        pl.semaphore_wait(barrier, 2 * plane + 1)

    @pl.when(outer)
    def _():
        for d in range(plane):
            greet({"expert": inner_base + ring[d]})
        pl.semaphore_wait(barrier, 2 * plane)

    def span(i):
        return pl.ds(i * part, part)

    def up_table(target, device):
        return remote(table, far_table.at[target], t_send.at[0], t_recv.at[target], device)

    def up_block(stream, i, target, device):
        source = (tok_hbm, grad_hbm)[stream]
        return remote(
            source.at[:, span(i)], land.at[target, stream, :, span(i)],
            x_send.at[0, stream, i], x_recv.at[target, stream, i], device,
        )

    def pass_table():
        return remote(far_table.at[0], far_table.at[2], t_send.at[1], t_recv.at[2], far_inner)

    def pass_block(stream, i):
        return remote(
            land.at[0, stream, :, span(i)], land.at[2, stream, :, span(i)],
            x_send.at[1, stream, i], x_recv.at[2, stream, i], far_inner,
        )

    def ups(target, device, streams=(0, 1)):
        return [up_block(stream, i, target, device) for stream in streams for i in range(PARTS)]

    @pl.when(inner)
    def _():
        start([up_table(1, far_inner), up_block(0, 0, 1, far_inner)])

    @pl.when(outer)
    def _():
        start([up_table(0, near_inner)] + ups(0, near_inner))

    swaps = [
        remote(src.at[0], dst.at[1], w_send.at[i], w_recv.at[i], twin)
        for i, (src, dst) in enumerate(weights)
    ]
    start(swaps)

    def tables(label, values, first, second, amount):
        count = amount * capacity
        p = lax.broadcasted_iota(jnp.int32, (amount, LANES), 0)
        expert = jnp.where(p < plane, first + p, second + p - plane).astype(jnp.float32)
        named = [jnp.where(values[k : k + 1] == expert, 1.0, 0.0) for k in range(2)]
        before = lax.broadcasted_iota(jnp.int32, (LANES, LANES), 0)
        after = lax.broadcasted_iota(jnp.int32, (LANES, LANES), 1)
        lower = jnp.where(before < after, 1.0, 0.0).astype(jnp.bfloat16)
        eye = jnp.where(before == after, 1.0, 0.0).astype(jnp.bfloat16)
        position = dot((named[0] + named[1]).astype(jnp.bfloat16), lower)
        place = lax.broadcasted_iota(jnp.int32, (amount, capacity, LANES), 1).astype(jnp.float32)
        hit = jnp.where(position[:, None, :] == place, 1.0, 0.0)
        chosen = [(hit * n[:, None, :]).reshape(count, LANES) for n in named]
        picks[label, :count] = (chosen[0] + chosen[1]).astype(jnp.bfloat16)
        weight = chosen[0] * values[2:3] + chosen[1] * values[3:4]
        high = weight.astype(jnp.bfloat16)
        low = (weight - high.astype(jnp.float32)).astype(jnp.bfloat16)
        for i, value in enumerate((high, low, *(c.astype(jnp.bfloat16) for c in chosen))):
            mats[label, i, :, :count] = dot_nt(eye, value).astype(jnp.bfloat16)

    def deal_copies(label, stream, i, buf, shift):
        return [
            remote(
                send.at[buf, shift + ring[d], :, span(i)],
                rows_in.at[stream, label, col, :, span(i)],
                a_send.at[label, stream, i, 0, d], a_recv.at[label, stream, i, d],
                {"expert": my_base + ring[d]},
            )
            for d in range(1, plane)
        ]

    def deal_across(label, stream, i, buf):
        return [
            remote(
                send.at[buf, plane + ring[d], :, span(i)],
                rows_in.at[stream, label, col, :, span(i)],
                a_send.at[label, stream, i, 1, d], a_recv.at[label, stream, i, d],
                {"expert": outer_base + ring[d]},
            )
            for d in range(plane)
        ]

    def deal(label, stream, i, source, buf, shift, amount):
        pick = picks[label, : amount * capacity]

        @pl.loop(i * part // STEP, (i + 1) * part // STEP)
        def _(k):
            cols = pl.ds(pl.multiple_of(k * STEP, STEP), STEP)
            rows = dot(pick, source[:, cols])
            send[buf, shift : shift + amount, :, cols] = rows.reshape(
                amount, capacity, STEP
            ).astype(jnp.bfloat16)

        start(deal_copies(label, stream, i, buf, shift))
        if amount == 2 * plane:
            start(deal_across(label, stream, i, buf))
        rows_in[stream, label, col, :, span(i)] = send[buf, shift + col, :, span(i)]

    def dealt(label, stream, i):
        source = send.at[0, 0, :, span(i)]
        target = rows_in.at[stream, label, 0, :, span(i)]

        def copy(d):
            return remote(
                source, target, a_send.at[label, stream, i, 0, d], a_recv.at[label, stream, i, d],
                near_inner,
            )

        arrived([copy(d) for d in range(1, plane)])
        if label != O:

            @pl.when(outer)
            def _():
                copy(0).wait_recv()

    def rows_of(buffer, cols):
        value = buffer[..., cols].astype(jnp.float32)
        return value.reshape(-1, value.shape[-1]).astype(jnp.bfloat16)

    def sums_for(labels):
        first = min(labels[0], FI) * block
        return slice(first, first + len(labels) * block)

    def front_in(labels, i):
        count, sums = len(labels) * block, sums_for(labels)
        if i == 0:
            acc[0, :, sums] = jnp.zeros((2, count, acc.shape[3]), jnp.float32)
            acc[1, :, sums] = jnp.zeros((2, count, acc.shape[3]), jnp.float32)

        @pl.loop(i * part // STEP, (i + 1) * part // STEP)
        def _(k):
            cols = pl.ds(pl.multiple_of(k * STEP, STEP), STEP)
            rows = rows_of(rows_in.at[0, labels[0] : labels[-1] + 1], cols)
            for j in range(2):
                acc[0, j, sums] += dot(rows, gate_w[j, cols, :])
                acc[1, j, sums] += dot(rows, up_w[j, cols, :])

    def front_out(labels, i):
        count, sums = len(labels) * block, sums_for(labels)
        if i == 0:
            acc[2, :, sums] = jnp.zeros((2, count, acc.shape[3]), jnp.float32)

        @pl.loop(i * part // STEP, (i + 1) * part // STEP)
        def _(k):
            cols = pl.ds(pl.multiple_of(k * STEP, STEP), STEP)
            rows = rows_of(rows_in.at[1, labels[0] : labels[-1] + 1], cols)
            for j in range(2):
                acc[2, j, sums] += dot_nt(rows, down_w[j, :, cols])

    def rows_for(labels):
        return slice(labels[0] * block, (labels[-1] + 1) * block)

    def pointwise(labels):
        count, rows = len(labels) * block, rows_for(labels)
        prob = jnp.zeros((count, 1), jnp.float32)
        for j in range(2):
            gating, lifted, grad_hidden = (acc[a, j, sums_for(labels)] for a in range(3))
            sigmoid = jax.nn.sigmoid(gating)
            active = gating * sigmoid
            hidden = (active * lifted).astype(jnp.bfloat16)
            prob += jnp.sum(hidden.astype(jnp.float32) * grad_hidden, axis=1, keepdims=True)
            slope_term = sigmoid * (1.0 + gating * (1.0 - sigmoid))
            grad_hid[0, j, rows] = (grad_hidden * lifted * slope_term).astype(jnp.bfloat16)
            grad_hid[1, j, rows] = (grad_hidden * active).astype(jnp.bfloat16)
        wide = jnp.broadcast_to(prob, (count, LANES)).reshape(-1, plane, capacity, LANES)
        rows_in[0, labels[0] : labels[-1] + 1, :, :, width:] = wide.astype(jnp.bfloat16)

    def slab(c):
        return pl.ds(c * piece, piece + (full - width if c == PIECES - 1 else 0))

    def home_copies(label, c):
        return [
            remote(
                rows_in.at[0, label, ring[d], :, slab(c)], back_in.at[label, col, :, slab(c)],
                b_send.at[label, c, 0, d], b_recv.at[label, c, 0, d],
                {"expert": my_base + ring[d]},
            )
            for d in range(1, plane)
        ]

    def home(labels, c):
        rows = rows_for(labels)

        @pl.loop(c * piece // STEP, (c + 1) * piece // STEP)
        def _(k):
            cols = pl.ds(pl.multiple_of(k * STEP, STEP), STEP)
            total = dot_nt(grad_hid[0, 0, rows], gate_w[0, cols, :])
            total += dot_nt(grad_hid[0, 1, rows], gate_w[1, cols, :])
            total += dot_nt(grad_hid[1, 0, rows], up_w[0, cols, :])
            total += dot_nt(grad_hid[1, 1, rows], up_w[1, cols, :])
            rows_in[0, labels[0] : labels[-1] + 1, :, :, cols] = total.reshape(
                len(labels), plane, capacity, STEP
            ).astype(jnp.bfloat16)

    def go_home(labels, c):
        for label in labels:
            start(home_copies(label, c))
            back_in[label, col, :, slab(c)] = rows_in[0, label, col, :, slab(c)]

    def relay_copy(label, c):
        return remote(
            back_in.at[label, :plane, :, slab(c)], back_in.at[label, plane:, :, slab(c)],
            b_send.at[label, c, 1, 0], b_recv.at[label, c, 1, 0], near_inner,
        )

    def relay(label):
        @pl.when(outer)
        def _():
            for c in pieces:
                arrived(home_copies(label, c))
                relay_copy(label, c).start()

    def homed(label, c):
        arrived(home_copies(label, c))
        if label != O:
            relay_copy(label, c).wait_recv()

    def combine(label, c, amount, extra, target, values):
        count = amount * capacity

        @pl.loop(c * piece // STEP, (c + 1) * piece // STEP)
        def _(k):
            cols = pl.ds(pl.multiple_of(k * STEP, STEP), STEP)
            rows = rows_of(back_in.at[label, :amount], cols)
            total = dot(mats[label, 0, :, :count], rows) + dot(mats[label, 1, :, :count], rows)
            if extra is not None:
                total += extra[:, cols].astype(jnp.float32)
            target[:, cols] = total.astype(jnp.bfloat16)

        if c == PIECES - 1:
            rows = rows_of(back_in.at[label, :amount], pl.ds(width, LANES))
            lane = lax.broadcasted_iota(jnp.int32, (LANES, LANES), 1)
            total = jnp.where(
                lane < LANES // 2,
                dot(mats[label, 2, :, :count], rows),
                dot(mats[label, 3, :, :count], rows),
            )
            if extra is not None:
                total += extra[:, width:].astype(jnp.float32)
            if values is None:
                half = LANES // 2
                row = lax.broadcasted_iota(jnp.int32, (8, LANES), 0)
                column = lax.broadcasted_iota(jnp.int32, (8, LANES), 1)
                first = jnp.where(column == row * half, 1.0, 0.0).astype(jnp.bfloat16)
                turned = dot_nt(first, total.astype(jnp.bfloat16))
                probs_out[...] = turned[:2].astype(jnp.bfloat16)
            else:
                values[...] = total.astype(jnp.bfloat16)

    def partial(which, c):
        return remote(
            land.at[1 + which, 0, :, slab(c)], part_in.at[which, :, slab(c)],
            p_send.at[which, c], p_recv.at[which, c], far_inner,
        )

    def last_hop(c):
        return remote(
            land.at[0, 0, :, slab(c)], land.at[0, 0, :, slab(c)], p_send.at[2, c], p_recv.at[2, c],
            near_outer,
        )

    def value_columns(ref):
        return ref.at[:, width:]

    parts, pieces, streams = range(PARTS), range(PIECES), range(2)

    @pl.when(inner)
    def _():
        tables(I, table[...], inner_base, outer_base, 2 * plane)

    @pl.when(outer)
    def _():
        tables(O, table[...], my_base, my_base, plane)

    for stream in streams:
        blocks[stream].wait()

        @pl.when(inner)
        def _():
            for i in parts:
                deal(I, stream, i, own.at[stream], stream, 0, 2 * plane)

        @pl.when(outer)
        def _():
            for i in parts:
                deal(O, stream, i, own.at[stream], stream, 0, plane)

    def own_sent():
        @pl.when(inner)
        def _():
            sent([up_table(1, far_inner)] + ups(1, far_inner))

    def cross_rest():
        @pl.when(inner)
        def _():
            for stream in streams:
                for i in parts:
                    if stream or i:
                        up_block(stream, i, 1, far_inner).start()

    def pass_outer(stream, some):
        @pl.when(inner)
        def _():
            for i in some:
                up_block(stream, i, 0, near_inner).wait_recv()
                pass_block(stream, i).start()
                deal(O, stream, i, land.at[0, stream], 4, stream * plane, plane)

    def deal_far(label, target, stream, buf, some):
        @pl.when(inner)
        def _():
            for i in some:
                up_block(stream, i, target, far_inner).wait_recv()
                deal(label, stream, i, land.at[target, stream], buf, 0, 2 * plane)

    def pass_and_deal():
        for i in parts:
            pass_outer(1, (i,))
            deal_far(FO, 2, 0, 2, (i,))

    def outer_tables():
        @pl.when(inner)
        def _():
            up_table(0, near_inner).wait_recv()
            pass_table().start()
            tables(O, far_table[0], my_base, my_base, plane)

    def far_tables(label):
        @pl.when(inner)
        def _():
            up_table(label - 1, far_inner).wait_recv()
            tables(label, far_table[label - 1], inner_base, outer_base, 2 * plane)

    def own_dealt():
        @pl.when(inner)
        def _():
            for stream in streams:
                for i in parts:
                    sent(deal_copies(I, stream, i, stream, 0) + deal_across(I, stream, i, stream))

    near = (I, O)

    def take_weights():
        for copy in locals_:
            copy.wait()
        arrived(swaps)

    def front(labels):
        for i in parts:
            for label in labels:
                dealt(label, 0, i)
            front_in(labels, i)

    def finish(labels):
        for i in parts:
            for label in labels:
                dealt(label, 1, i)
            front_out(labels, i)
        pointwise(labels)

    def make_home(labels):
        for c in pieces:
            home(labels, c)

    def start_home(labels):
        for c in pieces:
            go_home(labels, c)

    def send_home(labels):
        for c in pieces:
            home(labels, c)
            go_home(labels, c)

    def cross_back(label, which, some):
        @pl.when(inner)
        def _():
            target = land.at[1 + which, 0]
            for c in some:
                homed(label, c)
                combine(label, c, 2 * plane, None, target, value_columns(target))
                partial(which, c).start()

    def own_result():
        @pl.when(inner)
        def _():
            for c in pieces:
                homed(I, c)
                partial(0, c).wait_recv()
                combine(I, c, 2 * plane, part_in.at[0], out, None)

    def passed():
        @pl.when(inner)
        def _():
            for i in parts:
                pass_block(0, i).wait_send()

    def inward_result(some):
        @pl.when(inner)
        def _():
            for c in some:
                homed(O, c)
                partial(1, c).wait_recv()
                combine(O, c, plane, part_in.at[1], land.at[0, 0], value_columns(land.at[0, 0]))
                last_hop(c).start()

    def outer_result():
        @pl.when(outer)
        def _():
            for c in pieces:
                homed(O, c)
                last_hop(c).wait_recv()
                combine(O, c, plane, land.at[0, 0], out, None)

    def both_results():
        for c in pieces:
            inward_result((c,))
            cross_back(FI, 0, (c,))

    outer_tables()
    pass_outer(0, parts)
    far_tables(FO)
    pass_and_deal()
    cross_rest()
    take_weights()
    front(near)
    deal_far(FO, 2, 1, 3, parts)
    finish(near)
    make_home(near)
    start_home((O,))
    front((FO,))
    finish((FO,))
    send_home((FO,))
    far_tables(FI)
    own_dealt()
    deal_far(FI, 1, 0, 0, parts)
    relay(FO)
    front((FI,))
    start_home((I,))
    relay(I)
    cross_back(FO, 1, pieces)
    deal_far(FI, 1, 1, 1, parts)
    finish((FI,))
    send_home((FI,))
    relay(FI)
    passed()
    both_results()
    outer_result()
    own_result()
    own_sent()

    @pl.when(inner)
    def _():
        pass_table().wait_send()
        sent([pass_block(1, i) for i in parts])
        for stream in streams:
            for i in parts:
                sent(deal_copies(O, stream, i, 4, stream * plane))
                for label, buf in ((FI, 0), (FO, 2)):
                    sent(deal_copies(label, stream, i, buf + stream, 0))
                    sent(deal_across(label, stream, i, buf + stream))
        for c in pieces:
            for label in (I, FI, FO):
                sent(home_copies(label, c))
            sent([partial(0, c), partial(1, c), last_hop(c)])

    @pl.when(outer)
    def _():
        sent([up_table(0, near_inner)] + ups(0, near_inner))
        for stream in streams:
            for i in parts:
                sent(deal_copies(O, stream, i, stream, 0))
        for c in pieces:
            for label in (I, FI, FO):
                sent([*home_copies(label, c), relay_copy(label, c)])

    for c in pieces:
        sent(home_copies(O, c))
    sent(swaps)


def fused_on_device(tokens, routes, route_probs, gate_weight, up_weight, down_weight, grad_out):
    tok_count, width = tokens.shape
    top_count = routes.shape[1]
    experts = lax.axis_size("expert")
    capacity = 3 * tok_count * top_count // (2 * experts)
    plane = experts // LAYERS
    hid = gate_weight.shape[2]
    full = width + LANES
    bf16, f32 = jnp.bfloat16, jnp.float32
    vmem, sems = pltpu.VMEM, pltpu.SemaphoreType.DMA
    spec = pl.BlockSpec(memory_space=pltpu.VMEM)
    raw = pl.BlockSpec(memory_space=pl.ANY)
    grad_tokens, values = pl.pallas_call(
        lambda *refs: fused_kernel(plane, *refs),
        name="routed_backward",
        out_shape=(
            jax.ShapeDtypeStruct((tok_count, width), bf16),
            jax.ShapeDtypeStruct((top_count, tok_count), bf16),
        ),
        in_specs=[spec] * 2 + [raw] * 5,
        out_specs=(spec, spec),
        scratch_shapes=[
            vmem((8, tok_count), f32),
            vmem((2, tok_count, width), bf16),
            vmem((4, 2 * plane * capacity, tok_count), bf16),
            vmem((4, 4, tok_count, 2 * plane * capacity), bf16),
            vmem((3, 8, tok_count), f32),
            vmem((3, 2, tok_count, full), bf16),
            vmem((2, width, hid), bf16),
            vmem((2, width, hid), bf16),
            vmem((2, hid, width), bf16),
            vmem((5, 2 * plane, capacity, width), bf16),
            vmem((2, 4, plane, capacity, full), bf16),
            vmem((3, 2, 3 * plane * capacity, hid), f32),
            vmem((2, 2, 4 * plane * capacity, hid), bf16),
            vmem((4, 2 * plane, capacity, full), bf16),
            vmem((2, tok_count, full), bf16),
            sems((5,)),
            sems((3,)), sems((3,)),
            sems((2,)), sems((3,)),
            sems((2, 2, PARTS)), sems((3, 2, PARTS)),
            sems((4, 2, PARTS, 2, plane)), sems((4, 2, PARTS, plane)),
            sems((4, PIECES, 2, plane)), sems((4, PIECES, 2, plane)),
            sems((3, PIECES)), sems((3, PIECES)),
        ],
        compiler_params=pltpu.CompilerParams(
            collective_id=0, has_side_effects=True, vmem_limit_bytes=63 * 1024 * 1024
        ),
    )(routes.T, route_probs.T, tokens, grad_out, gate_weight, up_weight, down_weight)
    return grad_tokens, values.T


def on_device(tokens, routes, *rest):
    experts = lax.axis_size("expert")
    capacity = 3 * routes.shape[0] * routes.shape[1] // (2 * experts)
    fits = capacity % 8 == 0 and lax.axis_size("seq") == 2 and routes.shape[1] == 2
    fits = fits and experts == LAYERS * (experts // LAYERS) and routes.shape[0] == LANES
    run = fused_on_device if fits else halves_on_device
    return run(tokens, routes, *rest)


def solution(mesh):
    placed = (
        P(("seq", "expert"), None),
        P(("seq", "expert"), None),
        P(("seq", "expert"), None),
        P("expert", None, "seq"),
        P("expert", None, "seq"),
        P("expert", "seq", None),
        P(("seq", "expert"), None),
    )
    return jax.shard_map(
        on_device,
        mesh=mesh,
        in_specs=placed,
        out_specs=(P(("seq", "expert"), None), P(("seq", "expert"), None)),
        check_vma=False,
    )
```

```python
import jax
import jax.numpy as jnp
from jax import lax
from jax.experimental import pallas as pl
from jax.experimental.pallas import tpu as pltpu
from jax.sharding import PartitionSpec as P

CHUNKS = 2
PIECES = 8
PARTS = 4
LAYERS = 4
LANES = 128
I, O, FI, FO = range(4)
LEAD = 1
WIDE = 1024
STEP = 512
MESH = pl.DeviceIdType.MESH
NT = (((1,), (1,)), ((), ()))


def dot(a, b):
    return jnp.dot(a, b, preferred_element_type=jnp.float32)


def dot_nt(a, b):
    return lax.dot_general(a, b, NT, preferred_element_type=jnp.float32)


def slots_of(routes, base, half, capacity):
    local = routes - base
    chosen = local.reshape(-1)
    order = jnp.arange(chosen.shape[0], dtype=jnp.int32)
    earlier = (chosen[:, None] == chosen[None, :]) & (order[None, :] < order[:, None])
    position = jnp.sum(earlier.astype(jnp.int32), axis=1).reshape(routes.shape)
    valid = (local >= 0) & (local < half)
    return jnp.where(valid, local * capacity + position, -1)


def dispatch_of(slots, count):
    lanes = jnp.arange(count, dtype=jnp.int32)[:, None, None]
    return jnp.any(lanes == slots[None], axis=2).astype(jnp.bfloat16)


def weighting_of(slots, probs, count):
    lanes = jnp.arange(count, dtype=jnp.int32)[None, None, :]
    full = jnp.sum(jnp.where(slots[:, :, None] == lanes, probs[:, :, None], 0.0), axis=1)
    high = lax.reduce_precision(full, 8, 7)
    return high.astype(jnp.bfloat16), (full - high).astype(jnp.bfloat16)


def combine(weighting, rows):
    return dot(weighting[0], rows) + dot(weighting[1], rows)


def pick(slots, values):
    lanes = jnp.arange(values.shape[0], dtype=jnp.int32)[None, None, :]
    return jnp.sum(jnp.where(slots[:, :, None] == lanes, values[None, None, :], 0.0), axis=2)


def front(rows_in, gates, ups):
    return [(dot(rows_in, g), dot(rows_in, u)) for g, u in zip(gates, ups)]


def middle(terms, rows_grad, downs):
    prob, grads = 0.0, []
    for (gating, lifted), d in zip(terms, downs):
        sigmoid = jax.nn.sigmoid(gating)
        active = gating * sigmoid
        hidden = (active * lifted).astype(jnp.bfloat16)
        grad_hidden = dot_nt(rows_grad, d)
        prob = prob + jnp.sum(hidden.astype(jnp.float32) * grad_hidden, axis=1)
        slope_term = sigmoid * (1.0 + gating * (1.0 - sigmoid))
        grads.append(
            (
                (grad_hidden * lifted * slope_term).astype(jnp.bfloat16),
                (grad_hidden * active).astype(jnp.bfloat16),
            )
        )
    return grads, prob


def back(grads, gates, ups, columns):
    total = 0.0
    for (gg, gu), g, u in zip(grads, gates, ups):
        total = total + dot_nt(gg, g[columns]) + dot_nt(gu, u[columns])
    return total.astype(jnp.bfloat16)


def halves_on_device(tokens, routes, route_probs, gate_weight, up_weight, down_weight, grad_out):
    tok_count, width = tokens.shape
    top_count = routes.shape[1]
    experts = lax.axis_size("expert")
    parts = lax.axis_size("seq")
    capacity = 3 * tok_count * top_count // (2 * experts)
    half = experts // 2
    count = half * capacity
    base = (lax.axis_index("expert") // half) * half
    swap = [(i, (i + half) % experts) for i in range(experts)]
    groups = [list(range(half)), list(range(half, experts))]

    def across(value):
        return lax.ppermute(value, "expert", swap)

    def exchange(value):
        value = value.reshape(half, capacity, -1)
        value = lax.all_to_all(
            value, "expert", split_axis=0, concat_axis=0, tiled=True, axis_index_groups=groups
        )
        return value.reshape(count, -1)

    far_routes, far_probs = across(routes), across(route_probs)
    far_tokens, far_grad = across(tokens), across(grad_out)

    gates, ups, downs = [gate_weight[0]], [up_weight[0]], [down_weight[0]]
    for shift in range(1, parts):
        turn = [(i, (i + shift) % parts) for i in range(parts)]
        gates.append(lax.ppermute(gate_weight[0], "seq", turn))
        ups.append(lax.ppermute(up_weight[0], "seq", turn))
        downs.append(lax.ppermute(down_weight[0], "seq", turn))

    near_slots = slots_of(routes, base, half, capacity)
    near_pick = dispatch_of(near_slots, count)
    near_in = exchange(dot(near_pick, tokens).astype(jnp.bfloat16))
    near_out = exchange(dot(near_pick, grad_out).astype(jnp.bfloat16))
    near_grads, near_prob = middle(front(near_in, gates, ups), near_out, downs)

    far_slots = slots_of(far_routes, base, half, capacity)
    far_pick = dispatch_of(far_slots, count)
    far_in = exchange(dot(far_pick, far_tokens).astype(jnp.bfloat16))
    far_terms = front(far_in, gates, ups)
    far_out = exchange(dot(far_pick, far_grad).astype(jnp.bfloat16))
    far_grads, far_prob = middle(far_terms, far_out, downs)

    near_weighting = weighting_of(near_slots, route_probs, count)
    far_weighting = weighting_of(far_slots, far_probs, count)

    size = width // CHUNKS
    spans = [slice(c * size, (c + 1) * size) for c in range(CHUNKS)]

    def send_back(grads, prob, span):
        rows = back(grads, gates, ups, span)
        if span.start == 0:
            column = jnp.broadcast_to(prob.astype(jnp.bfloat16)[:, None], (count, 128))
            rows = jnp.concatenate([rows, column], axis=1)
        return exchange(rows)

    returned = []
    for span in spans:
        rows = send_back(far_grads, far_prob, span)
        partial = combine(far_weighting, rows[:, :size]).astype(jnp.bfloat16)
        returned.append(across(partial))
        if span.start == 0:
            far_values = pick(far_slots, rows[:, size].astype(jnp.float32))
            far_values = across(far_values.astype(jnp.bfloat16))
    pieces = []
    for span, far_piece in zip(spans, returned):
        rows = send_back(near_grads, near_prob, span)
        near_piece = combine(near_weighting, rows[:, :size])
        pieces.append((near_piece + far_piece.astype(jnp.float32)).astype(jnp.bfloat16))
        if span.start == 0:
            near_values = pick(near_slots, rows[:, size].astype(jnp.float32))
    grad_probs = (near_values + far_values.astype(jnp.float32)).astype(jnp.bfloat16)
    return (jnp.concatenate(pieces, axis=1), grad_probs)


def fused_kernel(
    plane,
    routes, probs, tok_hbm, grad_hbm, gate_hbm, up_hbm, down_hbm,
    out, probs_out,
    table, own, picks, mats, far_table, land, gate_w, up_w, down_w, send, rows_in, acc, grad_hid, back_in,
    part_in,
    local_sem, w_send, w_recv, t_send, t_recv, x_send, x_recv, a_send, a_recv, b_send, b_recv,
    p_send, p_recv,
):
    width, capacity = own.shape[2], send.shape[2]
    full = land.shape[3]
    block = plane * capacity
    piece, part = width // PIECES, width // PARTS
    me = lax.axis_index("expert")
    core = lax.axis_index("seq")
    layer = me // plane
    col = me - layer * plane
    side = layer // (LAYERS // 2)
    inner = (layer == 1) | (layer == 2)
    outer = jnp.logical_not(inner)
    my_base, inner_base = layer * plane, (side + 1) * plane
    outer_base = side * (LAYERS - 1) * plane
    twin = {"seq": 1 - core}
    near_inner = {"expert": inner_base + col}
    near_outer = {"expert": outer_base + col}
    far_inner = {"expert": (2 - side) * plane + col}
    ring = [lax.rem(col + d, plane) for d in range(plane)]

    def remote(src, dst, ss, rs, device):
        return pltpu.make_async_remote_copy(
            src_ref=src, dst_ref=dst, send_sem=ss, recv_sem=rs,
            device_id=device, device_id_type=MESH,
        )

    def start(copies):
        for copy in copies:
            copy.start()

    def arrived(copies):
        for copy in copies:
            copy.wait_recv()

    def sent(copies):
        for copy in copies:
            copy.wait_send()

    weights = ((gate_hbm, gate_w), (up_hbm, up_w), (down_hbm, down_w))
    blocks = [
        pltpu.make_async_copy(src, own.at[i], local_sem.at[i])
        for i, src in enumerate((tok_hbm, grad_hbm))
    ]
    locals_ = [
        pltpu.make_async_copy(src.at[0], dst.at[0], local_sem.at[2 + i])
        for i, (src, dst) in enumerate(weights)
    ]
    start(blocks + locals_)

    table[:2] = routes[...].astype(jnp.float32)
    table[2:4] = probs[...]
    table[4:] = jnp.zeros((4, LANES), jnp.float32)
    barrier = pltpu.get_barrier_semaphore()

    def greet(device):
        pl.semaphore_signal(barrier, inc=1, device_id=device, device_id_type=MESH)

    greet(twin)
    for d in range(1, plane):
        greet({"expert": my_base + ring[d]})

    @pl.when(inner)
    def _():
        greet(far_inner)
        for d in range(plane):
            greet({"expert": outer_base + ring[d]})
        pl.semaphore_wait(barrier, 2 * plane + 1)

    @pl.when(outer)
    def _():
        for d in range(plane):
            greet({"expert": inner_base + ring[d]})
        pl.semaphore_wait(barrier, 2 * plane)

    def span(i):
        return pl.ds(i * part, part)

    def up_table(target, device):
        return remote(table, far_table.at[target], t_send.at[0], t_recv.at[target], device)

    def up_block(stream, i, target, device):
        source = (tok_hbm, grad_hbm)[stream]
        return remote(
            source.at[:, span(i)], land.at[target, stream, :, span(i)],
            x_send.at[0, stream, i], x_recv.at[target, stream, i], device,
        )

    def pass_table():
        return remote(far_table.at[0], far_table.at[2], t_send.at[1], t_recv.at[2], far_inner)

    def pass_block(stream, i):
        return remote(
            land.at[0, stream, :, span(i)], land.at[2, stream, :, span(i)],
            x_send.at[1, stream, i], x_recv.at[2, stream, i], far_inner,
        )

    def ups(target, device, streams=(0, 1)):
        return [up_block(stream, i, target, device) for stream in streams for i in range(PARTS)]

    @pl.when(inner)
    def _():
        start([up_table(1, far_inner)] + [up_block(0, i, 1, far_inner) for i in range(LEAD)])

    @pl.when(outer)
    def _():
        start([up_table(0, near_inner)] + ups(0, near_inner))

    swaps = [
        remote(src.at[0], dst.at[1], w_send.at[i], w_recv.at[i], twin)
        for i, (src, dst) in enumerate(weights)
    ]
    start(swaps)

    def tables(label, values, first, second, amount):
        count = amount * capacity
        p = lax.broadcasted_iota(jnp.int32, (amount, LANES), 0)
        expert = jnp.where(p < plane, first + p, second + p - plane).astype(jnp.float32)
        named = [jnp.where(values[k : k + 1] == expert, 1.0, 0.0) for k in range(2)]
        before = lax.broadcasted_iota(jnp.int32, (LANES, LANES), 0)
        after = lax.broadcasted_iota(jnp.int32, (LANES, LANES), 1)
        lower = jnp.where(before < after, 1.0, 0.0).astype(jnp.bfloat16)
        eye = jnp.where(before == after, 1.0, 0.0).astype(jnp.bfloat16)
        position = dot((named[0] + named[1]).astype(jnp.bfloat16), lower)
        place = lax.broadcasted_iota(jnp.int32, (amount, capacity, LANES), 1).astype(jnp.float32)
        hit = jnp.where(position[:, None, :] == place, 1.0, 0.0)
        chosen = [(hit * n[:, None, :]).reshape(count, LANES) for n in named]
        picks[label, :count] = (chosen[0] + chosen[1]).astype(jnp.bfloat16)
        weight = chosen[0] * values[2:3] + chosen[1] * values[3:4]
        high = weight.astype(jnp.bfloat16)
        low = (weight - high.astype(jnp.float32)).astype(jnp.bfloat16)
        for i, value in enumerate((high, low, *(c.astype(jnp.bfloat16) for c in chosen))):
            mats[label, i, :, :count] = dot_nt(eye, value).astype(jnp.bfloat16)

    def deal_copies(label, stream, i, buf, shift):
        return [
            remote(
                send.at[buf, shift + ring[d], :, span(i)],
                rows_in.at[stream, label, col, :, span(i)],
                a_send.at[label, stream, i, 0, d], a_recv.at[label, stream, i, d],
                {"expert": my_base + ring[d]},
            )
            for d in range(1, plane)
        ]

    def deal_across(label, stream, i, buf):
        return [
            remote(
                send.at[buf, plane + ring[d], :, span(i)],
                rows_in.at[stream, label, col, :, span(i)],
                a_send.at[label, stream, i, 1, d], a_recv.at[label, stream, i, d],
                {"expert": outer_base + ring[d]},
            )
            for d in range(plane)
        ]

    def deal(label, stream, i, source, buf, shift, amount):
        pick = picks[label, : amount * capacity]

        @pl.loop(i * part // STEP, (i + 1) * part // STEP)
        def _(k):
            cols = pl.ds(pl.multiple_of(k * STEP, STEP), STEP)
            rows = dot(pick, source[:, cols])
            send[buf, shift : shift + amount, :, cols] = rows.reshape(
                amount, capacity, STEP
            ).astype(jnp.bfloat16)

        start(deal_copies(label, stream, i, buf, shift))
        if amount == 2 * plane:
            start(deal_across(label, stream, i, buf))
        rows_in[stream, label, col, :, span(i)] = send[buf, shift + col, :, span(i)]

    def dealt(label, stream, i):
        source = send.at[0, 0, :, span(i)]
        target = rows_in.at[stream, label, 0, :, span(i)]

        def copy(d):
            return remote(
                source, target, a_send.at[label, stream, i, 0, d], a_recv.at[label, stream, i, d],
                near_inner,
            )

        arrived([copy(d) for d in range(1, plane)])
        if label != O:

            @pl.when(outer)
            def _():
                copy(0).wait_recv()

    def rows_of(buffer, cols):
        value = buffer[..., cols].astype(jnp.float32)
        return value.reshape(-1, value.shape[-1]).astype(jnp.bfloat16)

    def sums_for(labels):
        first = min(labels[0], FI) * block
        return slice(first, first + len(labels) * block)

    def front_in(labels, i):
        count, sums = len(labels) * block, sums_for(labels)
        if i == 0:
            acc[0, :, sums] = jnp.zeros((2, count, acc.shape[3]), jnp.float32)
            acc[1, :, sums] = jnp.zeros((2, count, acc.shape[3]), jnp.float32)

        @pl.loop(i * part // WIDE, (i + 1) * part // WIDE)
        def _(k):
            cols = pl.ds(pl.multiple_of(k * WIDE, WIDE), WIDE)
            rows = rows_of(rows_in.at[0, labels[0] : labels[-1] + 1], cols)
            for j in range(2):
                acc[0, j, sums] += dot(rows, gate_w[j, cols, :])
                acc[1, j, sums] += dot(rows, up_w[j, cols, :])

    def front_out(labels, i):
        count, sums = len(labels) * block, sums_for(labels)
        if i == 0:
            acc[2, :, sums] = jnp.zeros((2, count, acc.shape[3]), jnp.float32)

        @pl.loop(i * part // WIDE, (i + 1) * part // WIDE)
        def _(k):
            cols = pl.ds(pl.multiple_of(k * WIDE, WIDE), WIDE)
            rows = rows_of(rows_in.at[1, labels[0] : labels[-1] + 1], cols)
            for j in range(2):
                acc[2, j, sums] += dot_nt(rows, down_w[j, :, cols])

    def rows_for(labels):
        return slice(labels[0] * block, (labels[-1] + 1) * block)

    def pointwise(labels):
        count, rows = len(labels) * block, rows_for(labels)
        prob = jnp.zeros((count, 1), jnp.float32)
        for j in range(2):
            gating, lifted, grad_hidden = (acc[a, j, sums_for(labels)] for a in range(3))
            sigmoid = jax.nn.sigmoid(gating)
            active = gating * sigmoid
            hidden = (active * lifted).astype(jnp.bfloat16)
            prob += jnp.sum(hidden.astype(jnp.float32) * grad_hidden, axis=1, keepdims=True)
            slope_term = sigmoid * (1.0 + gating * (1.0 - sigmoid))
            grad_hid[0, j, rows] = (grad_hidden * lifted * slope_term).astype(jnp.bfloat16)
            grad_hid[1, j, rows] = (grad_hidden * active).astype(jnp.bfloat16)
        wide = jnp.broadcast_to(prob, (count, LANES)).reshape(-1, plane, capacity, LANES)
        rows_in[0, labels[0] : labels[-1] + 1, :, :, width:] = wide.astype(jnp.bfloat16)

    def slab(c):
        return pl.ds(c * piece, piece + (full - width if c == PIECES - 1 else 0))

    def home_copies(label, c):
        return [
            remote(
                rows_in.at[0, label, ring[d], :, slab(c)], back_in.at[label, col, :, slab(c)],
                b_send.at[label, c, 0, d], b_recv.at[label, c, 0, d],
                {"expert": my_base + ring[d]},
            )
            for d in range(1, plane)
        ]

    def home(labels, c):
        rows = rows_for(labels)

        @pl.loop(c * piece // STEP, (c + 1) * piece // STEP)
        def _(k):
            cols = pl.ds(pl.multiple_of(k * STEP, STEP), STEP)
            total = dot_nt(grad_hid[0, 0, rows], gate_w[0, cols, :])
            total += dot_nt(grad_hid[0, 1, rows], gate_w[1, cols, :])
            total += dot_nt(grad_hid[1, 0, rows], up_w[0, cols, :])
            total += dot_nt(grad_hid[1, 1, rows], up_w[1, cols, :])
            rows_in[0, labels[0] : labels[-1] + 1, :, :, cols] = total.reshape(
                len(labels), plane, capacity, STEP
            ).astype(jnp.bfloat16)

    def go_home(labels, c):
        for label in labels:
            start(home_copies(label, c))
            back_in[label, col, :, slab(c)] = rows_in[0, label, col, :, slab(c)]

    def relay_copy(label, c):
        return remote(
            back_in.at[label, :plane, :, slab(c)], back_in.at[label, plane:, :, slab(c)],
            b_send.at[label, c, 1, 0], b_recv.at[label, c, 1, 0], near_inner,
        )

    def relay(label):
        @pl.when(outer)
        def _():
            for c in pieces:
                arrived(home_copies(label, c))
                relay_copy(label, c).start()

    def homed(label, c):
        arrived(home_copies(label, c))
        if label != O:
            relay_copy(label, c).wait_recv()

    def combine(label, c, amount, extra, target, values):
        count = amount * capacity

        @pl.loop(c * piece // STEP, (c + 1) * piece // STEP)
        def _(k):
            cols = pl.ds(pl.multiple_of(k * STEP, STEP), STEP)
            rows = rows_of(back_in.at[label, :amount], cols)
            total = dot(mats[label, 0, :, :count], rows) + dot(mats[label, 1, :, :count], rows)
            if extra is not None:
                total += extra[:, cols].astype(jnp.float32)
            target[:, cols] = total.astype(jnp.bfloat16)

        if c == PIECES - 1:
            rows = rows_of(back_in.at[label, :amount], pl.ds(width, LANES))
            lane = lax.broadcasted_iota(jnp.int32, (LANES, LANES), 1)
            total = jnp.where(
                lane < LANES // 2,
                dot(mats[label, 2, :, :count], rows),
                dot(mats[label, 3, :, :count], rows),
            )
            if extra is not None:
                total += extra[:, width:].astype(jnp.float32)
            if values is None:
                half = LANES // 2
                row = lax.broadcasted_iota(jnp.int32, (8, LANES), 0)
                column = lax.broadcasted_iota(jnp.int32, (8, LANES), 1)
                first = jnp.where(column == row * half, 1.0, 0.0).astype(jnp.bfloat16)
                turned = dot_nt(first, total.astype(jnp.bfloat16))
                probs_out[...] = turned[:2].astype(jnp.bfloat16)
            else:
                values[...] = total.astype(jnp.bfloat16)

    def partial(which, c):
        return remote(
            land.at[1 + which, 0, :, slab(c)], part_in.at[which, :, slab(c)],
            p_send.at[which, c], p_recv.at[which, c], far_inner,
        )

    def last_hop(c):
        return remote(
            land.at[0, 0, :, slab(c)], land.at[0, 0, :, slab(c)], p_send.at[2, c], p_recv.at[2, c],
            near_outer,
        )

    def value_columns(ref):
        return ref.at[:, width:]

    parts, pieces, streams = range(PARTS), range(PIECES), range(2)

    @pl.when(inner)
    def _():
        tables(I, table[...], inner_base, outer_base, 2 * plane)

    @pl.when(outer)
    def _():
        tables(O, table[...], my_base, my_base, plane)

    for stream in streams:
        blocks[stream].wait()

        @pl.when(inner)
        def _():
            for i in parts:
                deal(I, stream, i, own.at[stream], stream, 0, 2 * plane)

        @pl.when(outer)
        def _():
            for i in parts:
                deal(O, stream, i, own.at[stream], stream, 0, plane)

    def own_sent():
        @pl.when(inner)
        def _():
            sent([up_table(1, far_inner)] + ups(1, far_inner))

    def cross_rest():
        @pl.when(inner)
        def _():
            for stream in streams:
                for i in parts:
                    if stream or i >= LEAD:
                        up_block(stream, i, 1, far_inner).start()

    def pass_outer(stream, some):
        @pl.when(inner)
        def _():
            for i in some:
                up_block(stream, i, 0, near_inner).wait_recv()
                pass_block(stream, i).start()
                deal(O, stream, i, land.at[0, stream], 4, stream * plane, plane)

    def deal_far(label, target, stream, buf, some):
        @pl.when(inner)
        def _():
            for i in some:
                up_block(stream, i, target, far_inner).wait_recv()
                deal(label, stream, i, land.at[target, stream], buf, 0, 2 * plane)

    def pass_and_deal():
        for i in parts:
            pass_outer(1, (i,))
            deal_far(FO, 2, 0, 2, (i,))

    def outer_tables():
        @pl.when(inner)
        def _():
            up_table(0, near_inner).wait_recv()
            pass_table().start()
            tables(O, far_table[0], my_base, my_base, plane)

    def far_tables(label):
        @pl.when(inner)
        def _():
            up_table(label - 1, far_inner).wait_recv()
            tables(label, far_table[label - 1], inner_base, outer_base, 2 * plane)

    def own_dealt():
        @pl.when(inner)
        def _():
            for stream in streams:
                for i in parts:
                    sent(deal_copies(I, stream, i, stream, 0) + deal_across(I, stream, i, stream))

    near = (I, O)

    def take_weights():
        for copy in locals_:
            copy.wait()
        arrived(swaps)

    def front(labels):
        for i in parts:
            for label in labels:
                dealt(label, 0, i)
            front_in(labels, i)

    def finish(labels):
        for i in parts:
            for label in labels:
                dealt(label, 1, i)
            front_out(labels, i)
        pointwise(labels)

    def make_home(labels):
        for c in pieces:
            home(labels, c)

    def start_home(labels):
        for c in pieces:
            go_home(labels, c)

    def send_home(labels):
        for c in pieces:
            home(labels, c)
            go_home(labels, c)

    def cross_back(label, which, some):
        @pl.when(inner)
        def _():
            target = land.at[1 + which, 0]
            for c in some:
                homed(label, c)
                combine(label, c, 2 * plane, None, target, value_columns(target))
                partial(which, c).start()

    def own_result():
        @pl.when(inner)
        def _():
            for c in pieces:
                homed(I, c)
                partial(0, c).wait_recv()
                combine(I, c, 2 * plane, part_in.at[0], out, None)

    def passed():
        @pl.when(inner)
        def _():
            for i in parts:
                pass_block(0, i).wait_send()

    def inward_result(some):
        @pl.when(inner)
        def _():
            for c in some:
                homed(O, c)
                partial(1, c).wait_recv()
                combine(O, c, plane, part_in.at[1], land.at[0, 0], value_columns(land.at[0, 0]))
                last_hop(c).start()

    def outer_result():
        @pl.when(outer)
        def _():
            for c in pieces:
                homed(O, c)
                last_hop(c).wait_recv()
                combine(O, c, plane, land.at[0, 0], out, None)

    def both_results():
        for c in pieces:
            inward_result((c,))
            cross_back(FI, 0, (c,))

    outer_tables()
    pass_outer(0, parts)
    far_tables(FO)
    pass_and_deal()
    cross_rest()
    take_weights()
    front(near)
    deal_far(FO, 2, 1, 3, parts)
    finish(near)
    make_home(near)
    start_home((O,))
    front((FO,))
    finish((FO,))
    send_home((FO,))
    far_tables(FI)
    own_dealt()
    deal_far(FI, 1, 0, 0, parts)
    relay(FO)
    front((FI,))
    start_home((I,))
    relay(I)
    deal_far(FI, 1, 1, 1, parts[:1])
    cross_back(FO, 1, pieces)
    deal_far(FI, 1, 1, 1, parts[1:])
    finish((FI,))
    send_home((FI,))
    relay(FI)
    passed()
    both_results()
    outer_result()
    own_result()
    own_sent()

    @pl.when(inner)
    def _():
        pass_table().wait_send()
        sent([pass_block(1, i) for i in parts])
        for stream in streams:
            for i in parts:
                sent(deal_copies(O, stream, i, 4, stream * plane))
                for label, buf in ((FI, 0), (FO, 2)):
                    sent(deal_copies(label, stream, i, buf + stream, 0))
                    sent(deal_across(label, stream, i, buf + stream))
        for c in pieces:
            for label in (I, FI, FO):
                sent(home_copies(label, c))
            sent([partial(0, c), partial(1, c), last_hop(c)])

    @pl.when(outer)
    def _():
        sent([up_table(0, near_inner)] + ups(0, near_inner))
        for stream in streams:
            for i in parts:
                sent(deal_copies(O, stream, i, stream, 0))
        for c in pieces:
            for label in (I, FI, FO):
                sent([*home_copies(label, c), relay_copy(label, c)])

    for c in pieces:
        sent(home_copies(O, c))
    sent(swaps)


def fused_on_device(tokens, routes, route_probs, gate_weight, up_weight, down_weight, grad_out):
    tok_count, width = tokens.shape
    top_count = routes.shape[1]
    experts = lax.axis_size("expert")
    capacity = 3 * tok_count * top_count // (2 * experts)
    plane = experts // LAYERS
    hid = gate_weight.shape[2]
    full = width + LANES
    bf16, f32 = jnp.bfloat16, jnp.float32
    vmem, sems = pltpu.VMEM, pltpu.SemaphoreType.DMA
    spec = pl.BlockSpec(memory_space=pltpu.VMEM)
    raw = pl.BlockSpec(memory_space=pl.ANY)
    grad_tokens, values = pl.pallas_call(
        lambda *refs: fused_kernel(plane, *refs),
        name="routed_backward",
        out_shape=(
            jax.ShapeDtypeStruct((tok_count, width), bf16),
            jax.ShapeDtypeStruct((top_count, tok_count), bf16),
        ),
        in_specs=[spec] * 2 + [raw] * 5,
        out_specs=(spec, spec),
        scratch_shapes=[
            vmem((8, tok_count), f32),
            vmem((2, tok_count, width), bf16),
            vmem((4, 2 * plane * capacity, tok_count), bf16),
            vmem((4, 4, tok_count, 2 * plane * capacity), bf16),
            vmem((3, 8, tok_count), f32),
            vmem((3, 2, tok_count, full), bf16),
            vmem((2, width, hid), bf16),
            vmem((2, width, hid), bf16),
            vmem((2, hid, width), bf16),
            vmem((5, 2 * plane, capacity, width), bf16),
            vmem((2, 4, plane, capacity, full), bf16),
            vmem((3, 2, 3 * plane * capacity, hid), f32),
            vmem((2, 2, 4 * plane * capacity, hid), bf16),
            vmem((4, 2 * plane, capacity, full), bf16),
            vmem((2, tok_count, full), bf16),
            sems((5,)),
            sems((3,)), sems((3,)),
            sems((2,)), sems((3,)),
            sems((2, 2, PARTS)), sems((3, 2, PARTS)),
            sems((4, 2, PARTS, 2, plane)), sems((4, 2, PARTS, plane)),
            sems((4, PIECES, 2, plane)), sems((4, PIECES, 2, plane)),
            sems((3, PIECES)), sems((3, PIECES)),
        ],
        compiler_params=pltpu.CompilerParams(
            collective_id=0, has_side_effects=True, vmem_limit_bytes=63 * 1024 * 1024
        ),
    )(routes.T, route_probs.T, tokens, grad_out, gate_weight, up_weight, down_weight)
    return grad_tokens, values.T


def on_device(tokens, routes, *rest):
    experts = lax.axis_size("expert")
    capacity = 3 * routes.shape[0] * routes.shape[1] // (2 * experts)
    fits = capacity % 8 == 0 and lax.axis_size("seq") == 2 and routes.shape[1] == 2
    fits = fits and experts == LAYERS * (experts // LAYERS) and routes.shape[0] == LANES
    run = fused_on_device if fits else halves_on_device
    return run(tokens, routes, *rest)


def solution(mesh):
    placed = (
        P(("seq", "expert"), None),
        P(("seq", "expert"), None),
        P(("seq", "expert"), None),
        P("expert", None, "seq"),
        P("expert", None, "seq"),
        P("expert", "seq", None),
        P(("seq", "expert"), None),
    )
    return jax.shard_map(
        on_device,
        mesh=mesh,
        in_specs=placed,
        out_specs=(P(("seq", "expert"), None), P(("seq", "expert"), None)),
        check_vma=False,
    )
```

```python
import jax
import jax.numpy as jnp
from jax import lax
from jax.experimental import pallas as pl
from jax.experimental.pallas import tpu as pltpu
from jax.sharding import PartitionSpec as P

CHUNKS = 2
PIECES = 8
PARTS = 4
LAYERS = 4
LANES = 128
I, O, FI, FO = range(4)
LEAD = 1
WIDE = 1024
STEP = 512
MESH = pl.DeviceIdType.MESH
NT = (((1,), (1,)), ((), ()))


def dot(a, b):
    return jnp.dot(a, b, preferred_element_type=jnp.float32)


def dot_nt(a, b):
    return lax.dot_general(a, b, NT, preferred_element_type=jnp.float32)


def slots_of(routes, base, half, capacity):
    local = routes - base
    chosen = local.reshape(-1)
    order = jnp.arange(chosen.shape[0], dtype=jnp.int32)
    earlier = (chosen[:, None] == chosen[None, :]) & (order[None, :] < order[:, None])
    position = jnp.sum(earlier.astype(jnp.int32), axis=1).reshape(routes.shape)
    valid = (local >= 0) & (local < half)
    return jnp.where(valid, local * capacity + position, -1)


def dispatch_of(slots, count):
    lanes = jnp.arange(count, dtype=jnp.int32)[:, None, None]
    return jnp.any(lanes == slots[None], axis=2).astype(jnp.bfloat16)


def weighting_of(slots, probs, count):
    lanes = jnp.arange(count, dtype=jnp.int32)[None, None, :]
    full = jnp.sum(jnp.where(slots[:, :, None] == lanes, probs[:, :, None], 0.0), axis=1)
    high = lax.reduce_precision(full, 8, 7)
    return high.astype(jnp.bfloat16), (full - high).astype(jnp.bfloat16)


def combine(weighting, rows):
    return dot(weighting[0], rows) + dot(weighting[1], rows)


def pick(slots, values):
    lanes = jnp.arange(values.shape[0], dtype=jnp.int32)[None, None, :]
    return jnp.sum(jnp.where(slots[:, :, None] == lanes, values[None, None, :], 0.0), axis=2)


def front(rows_in, gates, ups):
    return [(dot(rows_in, g), dot(rows_in, u)) for g, u in zip(gates, ups)]


def middle(terms, rows_grad, downs):
    prob, grads = 0.0, []
    for (gating, lifted), d in zip(terms, downs):
        sigmoid = jax.nn.sigmoid(gating)
        active = gating * sigmoid
        hidden = (active * lifted).astype(jnp.bfloat16)
        grad_hidden = dot_nt(rows_grad, d)
        prob = prob + jnp.sum(hidden.astype(jnp.float32) * grad_hidden, axis=1)
        slope_term = sigmoid * (1.0 + gating * (1.0 - sigmoid))
        grads.append(
            (
                (grad_hidden * lifted * slope_term).astype(jnp.bfloat16),
                (grad_hidden * active).astype(jnp.bfloat16),
            )
        )
    return grads, prob


def back(grads, gates, ups, columns):
    total = 0.0
    for (gg, gu), g, u in zip(grads, gates, ups):
        total = total + dot_nt(gg, g[columns]) + dot_nt(gu, u[columns])
    return total.astype(jnp.bfloat16)


def halves_on_device(tokens, routes, route_probs, gate_weight, up_weight, down_weight, grad_out):
    tok_count, width = tokens.shape
    top_count = routes.shape[1]
    experts = lax.axis_size("expert")
    parts = lax.axis_size("seq")
    capacity = 3 * tok_count * top_count // (2 * experts)
    half = experts // 2
    count = half * capacity
    base = (lax.axis_index("expert") // half) * half
    swap = [(i, (i + half) % experts) for i in range(experts)]
    groups = [list(range(half)), list(range(half, experts))]

    def across(value):
        return lax.ppermute(value, "expert", swap)

    def exchange(value):
        value = value.reshape(half, capacity, -1)
        value = lax.all_to_all(
            value, "expert", split_axis=0, concat_axis=0, tiled=True, axis_index_groups=groups
        )
        return value.reshape(count, -1)

    far_routes, far_probs = across(routes), across(route_probs)
    far_tokens, far_grad = across(tokens), across(grad_out)

    gates, ups, downs = [gate_weight[0]], [up_weight[0]], [down_weight[0]]
    for shift in range(1, parts):
        turn = [(i, (i + shift) % parts) for i in range(parts)]
        gates.append(lax.ppermute(gate_weight[0], "seq", turn))
        ups.append(lax.ppermute(up_weight[0], "seq", turn))
        downs.append(lax.ppermute(down_weight[0], "seq", turn))

    near_slots = slots_of(routes, base, half, capacity)
    near_pick = dispatch_of(near_slots, count)
    near_in = exchange(dot(near_pick, tokens).astype(jnp.bfloat16))
    near_out = exchange(dot(near_pick, grad_out).astype(jnp.bfloat16))
    near_grads, near_prob = middle(front(near_in, gates, ups), near_out, downs)

    far_slots = slots_of(far_routes, base, half, capacity)
    far_pick = dispatch_of(far_slots, count)
    far_in = exchange(dot(far_pick, far_tokens).astype(jnp.bfloat16))
    far_terms = front(far_in, gates, ups)
    far_out = exchange(dot(far_pick, far_grad).astype(jnp.bfloat16))
    far_grads, far_prob = middle(far_terms, far_out, downs)

    near_weighting = weighting_of(near_slots, route_probs, count)
    far_weighting = weighting_of(far_slots, far_probs, count)

    size = width // CHUNKS
    spans = [slice(c * size, (c + 1) * size) for c in range(CHUNKS)]

    def send_back(grads, prob, span):
        rows = back(grads, gates, ups, span)
        if span.start == 0:
            column = jnp.broadcast_to(prob.astype(jnp.bfloat16)[:, None], (count, 128))
            rows = jnp.concatenate([rows, column], axis=1)
        return exchange(rows)

    returned = []
    for span in spans:
        rows = send_back(far_grads, far_prob, span)
        partial = combine(far_weighting, rows[:, :size]).astype(jnp.bfloat16)
        returned.append(across(partial))
        if span.start == 0:
            far_values = pick(far_slots, rows[:, size].astype(jnp.float32))
            far_values = across(far_values.astype(jnp.bfloat16))
    pieces = []
    for span, far_piece in zip(spans, returned):
        rows = send_back(near_grads, near_prob, span)
        near_piece = combine(near_weighting, rows[:, :size])
        pieces.append((near_piece + far_piece.astype(jnp.float32)).astype(jnp.bfloat16))
        if span.start == 0:
            near_values = pick(near_slots, rows[:, size].astype(jnp.float32))
    grad_probs = (near_values + far_values.astype(jnp.float32)).astype(jnp.bfloat16)
    return (jnp.concatenate(pieces, axis=1), grad_probs)


def fused_kernel(
    plane,
    routes, probs, tok_hbm, grad_hbm, gate_hbm, up_hbm, down_hbm,
    out, probs_out,
    table, own, picks, mats, far_table, land, gate_w, up_w, down_w, send, rows_in, acc, grad_hid, back_in,
    part_in,
    local_sem, w_send, w_recv, t_send, t_recv, x_send, x_recv, a_send, a_recv, b_send, b_recv,
    p_send, p_recv,
):
    width, capacity = own.shape[2], send.shape[2]
    full = land.shape[3]
    block = plane * capacity
    piece, part = width // PIECES, width // PARTS
    me = lax.axis_index("expert")
    core = lax.axis_index("seq")
    layer = me // plane
    col = me - layer * plane
    side = layer // (LAYERS // 2)
    inner = (layer == 1) | (layer == 2)
    outer = jnp.logical_not(inner)
    my_base, inner_base = layer * plane, (side + 1) * plane
    outer_base = side * (LAYERS - 1) * plane
    twin = {"seq": 1 - core}
    near_inner = {"expert": inner_base + col}
    near_outer = {"expert": outer_base + col}
    far_inner = {"expert": (2 - side) * plane + col}
    ring = [lax.rem(col + d, plane) for d in range(plane)]

    def remote(src, dst, ss, rs, device):
        return pltpu.make_async_remote_copy(
            src_ref=src, dst_ref=dst, send_sem=ss, recv_sem=rs,
            device_id=device, device_id_type=MESH,
        )

    def start(copies):
        for copy in copies:
            copy.start()

    def arrived(copies):
        for copy in copies:
            copy.wait_recv()

    def sent(copies):
        for copy in copies:
            copy.wait_send()

    weights = ((gate_hbm, gate_w), (up_hbm, up_w), (down_hbm, down_w))
    blocks = [
        pltpu.make_async_copy(src, own.at[i], local_sem.at[i])
        for i, src in enumerate((tok_hbm, grad_hbm))
    ]
    locals_ = [
        pltpu.make_async_copy(src.at[0], dst.at[0], local_sem.at[2 + i])
        for i, (src, dst) in enumerate(weights)
    ]
    start(blocks + locals_)

    table[:2] = routes[...].astype(jnp.float32)
    table[2:4] = probs[...]
    table[4:] = jnp.zeros((4, LANES), jnp.float32)
    barrier = pltpu.get_barrier_semaphore()

    def greet(device):
        pl.semaphore_signal(barrier, inc=1, device_id=device, device_id_type=MESH)

    greet(twin)
    for d in range(1, plane):
        greet({"expert": my_base + ring[d]})

    @pl.when(inner)
    def _():
        greet(far_inner)
        for d in range(plane):
            greet({"expert": outer_base + ring[d]})
        pl.semaphore_wait(barrier, 2 * plane + 1)

    @pl.when(outer)
    def _():
        for d in range(plane):
            greet({"expert": inner_base + ring[d]})
        pl.semaphore_wait(barrier, 2 * plane)

    def span(i):
        return pl.ds(i * part, part)

    def up_table(target, device):
        return remote(table, far_table.at[target], t_send.at[0], t_recv.at[target], device)

    def up_block(stream, i, target, device):
        source = (tok_hbm, grad_hbm)[stream]
        return remote(
            source.at[:, span(i)], land.at[target, stream, :, span(i)],
            x_send.at[0, stream, i], x_recv.at[target, stream, i], device,
        )

    def pass_table():
        return remote(far_table.at[0], far_table.at[2], t_send.at[1], t_recv.at[2], far_inner)

    def pass_block(stream, i):
        return remote(
            land.at[0, stream, :, span(i)], land.at[2, stream, :, span(i)],
            x_send.at[1, stream, i], x_recv.at[2, stream, i], far_inner,
        )

    def ups(target, device, streams=(0, 1)):
        return [up_block(stream, i, target, device) for stream in streams for i in range(PARTS)]

    @pl.when(inner)
    def _():
        start([up_table(1, far_inner)] + [up_block(0, i, 1, far_inner) for i in range(LEAD)])

    @pl.when(outer)
    def _():
        start([up_table(0, near_inner)] + ups(0, near_inner))

    swaps = [
        remote(src.at[0], dst.at[1], w_send.at[i], w_recv.at[i], twin)
        for i, (src, dst) in enumerate(weights)
    ]
    start(swaps)

    def tables(label, values, first, second, amount):
        count = amount * capacity
        p = lax.broadcasted_iota(jnp.int32, (amount, LANES), 0)
        expert = jnp.where(p < plane, first + p, second + p - plane).astype(jnp.float32)
        named = [jnp.where(values[k : k + 1] == expert, 1.0, 0.0) for k in range(2)]
        before = lax.broadcasted_iota(jnp.int32, (LANES, LANES), 0)
        after = lax.broadcasted_iota(jnp.int32, (LANES, LANES), 1)
        lower = jnp.where(before < after, 1.0, 0.0).astype(jnp.bfloat16)
        eye = jnp.where(before == after, 1.0, 0.0).astype(jnp.bfloat16)
        position = dot((named[0] + named[1]).astype(jnp.bfloat16), lower)
        place = lax.broadcasted_iota(jnp.int32, (amount, capacity, LANES), 1).astype(jnp.float32)
        hit = jnp.where(position[:, None, :] == place, 1.0, 0.0)
        chosen = [(hit * n[:, None, :]).reshape(count, LANES) for n in named]
        picks[label, :count] = (chosen[0] + chosen[1]).astype(jnp.bfloat16)
        weight = chosen[0] * values[2:3] + chosen[1] * values[3:4]
        high = weight.astype(jnp.bfloat16)
        low = (weight - high.astype(jnp.float32)).astype(jnp.bfloat16)
        for i, value in enumerate((high, low, *(c.astype(jnp.bfloat16) for c in chosen))):
            mats[label, i, :, :count] = dot_nt(eye, value).astype(jnp.bfloat16)

    def deal_copies(label, stream, i, buf, shift):
        return [
            remote(
                send.at[buf, shift + ring[d], :, span(i)],
                rows_in.at[stream, label, col, :, span(i)],
                a_send.at[label, stream, i, 0, d], a_recv.at[label, stream, i, d],
                {"expert": my_base + ring[d]},
            )
            for d in range(1, plane)
        ]

    def deal_across(label, stream, i, buf):
        return [
            remote(
                send.at[buf, plane + ring[d], :, span(i)],
                rows_in.at[stream, label, col, :, span(i)],
                a_send.at[label, stream, i, 1, d], a_recv.at[label, stream, i, d],
                {"expert": outer_base + ring[d]},
            )
            for d in range(plane)
        ]

    def deal(label, stream, i, source, buf, shift, amount):
        pick = picks[label, : amount * capacity]

        @pl.loop(i * part // WIDE, (i + 1) * part // WIDE)
        def _(k):
            cols = pl.ds(pl.multiple_of(k * WIDE, WIDE), WIDE)
            rows = dot(pick, source[:, cols])
            send[buf, shift : shift + amount, :, cols] = rows.reshape(
                amount, capacity, WIDE
            ).astype(jnp.bfloat16)

        start(deal_copies(label, stream, i, buf, shift))
        if amount == 2 * plane:
            start(deal_across(label, stream, i, buf))
        rows_in[stream, label, col, :, span(i)] = send[buf, shift + col, :, span(i)]

    def dealt(label, stream, i):
        source = send.at[0, 0, :, span(i)]
        target = rows_in.at[stream, label, 0, :, span(i)]

        def copy(d):
            return remote(
                source, target, a_send.at[label, stream, i, 0, d], a_recv.at[label, stream, i, d],
                near_inner,
            )

        arrived([copy(d) for d in range(1, plane)])
        if label != O:

            @pl.when(outer)
            def _():
                copy(0).wait_recv()

    def rows_of(buffer, cols):
        value = buffer[..., cols].astype(jnp.float32)
        return value.reshape(-1, value.shape[-1]).astype(jnp.bfloat16)

    def sums_for(labels):
        first = min(labels[0], FI) * block
        return slice(first, first + len(labels) * block)

    def front_in(labels, i):
        count, sums = len(labels) * block, sums_for(labels)
        if i == 0:
            acc[0, :, sums] = jnp.zeros((2, count, acc.shape[3]), jnp.float32)
            acc[1, :, sums] = jnp.zeros((2, count, acc.shape[3]), jnp.float32)

        @pl.loop(i * part // WIDE, (i + 1) * part // WIDE)
        def _(k):
            cols = pl.ds(pl.multiple_of(k * WIDE, WIDE), WIDE)
            rows = rows_of(rows_in.at[0, labels[0] : labels[-1] + 1], cols)
            for j in range(2):
                acc[0, j, sums] += dot(rows, gate_w[j, cols, :])
                acc[1, j, sums] += dot(rows, up_w[j, cols, :])

    def front_out(labels, i):
        count, sums = len(labels) * block, sums_for(labels)
        if i == 0:
            acc[2, :, sums] = jnp.zeros((2, count, acc.shape[3]), jnp.float32)

        @pl.loop(i * part // WIDE, (i + 1) * part // WIDE)
        def _(k):
            cols = pl.ds(pl.multiple_of(k * WIDE, WIDE), WIDE)
            rows = rows_of(rows_in.at[1, labels[0] : labels[-1] + 1], cols)
            for j in range(2):
                acc[2, j, sums] += dot_nt(rows, down_w[j, :, cols])

    def rows_for(labels):
        return slice(labels[0] * block, (labels[-1] + 1) * block)

    def pointwise(labels):
        count, rows = len(labels) * block, rows_for(labels)
        prob = jnp.zeros((count, 1), jnp.float32)
        for j in range(2):
            gating, lifted, grad_hidden = (acc[a, j, sums_for(labels)] for a in range(3))
            sigmoid = jax.nn.sigmoid(gating)
            active = gating * sigmoid
            hidden = (active * lifted).astype(jnp.bfloat16)
            prob += jnp.sum(hidden.astype(jnp.float32) * grad_hidden, axis=1, keepdims=True)
            slope_term = sigmoid * (1.0 + gating * (1.0 - sigmoid))
            grad_hid[0, j, rows] = (grad_hidden * lifted * slope_term).astype(jnp.bfloat16)
            grad_hid[1, j, rows] = (grad_hidden * active).astype(jnp.bfloat16)
        wide = jnp.broadcast_to(prob, (count, LANES)).reshape(-1, plane, capacity, LANES)
        rows_in[0, labels[0] : labels[-1] + 1, :, :, width:] = wide.astype(jnp.bfloat16)

    def slab(c):
        return pl.ds(c * piece, piece + (full - width if c == PIECES - 1 else 0))

    def home_copies(label, c):
        return [
            remote(
                rows_in.at[0, label, ring[d], :, slab(c)], back_in.at[label, col, :, slab(c)],
                b_send.at[label, c, 0, d], b_recv.at[label, c, 0, d],
                {"expert": my_base + ring[d]},
            )
            for d in range(1, plane)
        ]

    def home(labels, c):
        rows = rows_for(labels)

        @pl.loop(c * piece // STEP, (c + 1) * piece // STEP)
        def _(k):
            cols = pl.ds(pl.multiple_of(k * STEP, STEP), STEP)
            total = dot_nt(grad_hid[0, 0, rows], gate_w[0, cols, :])
            total += dot_nt(grad_hid[0, 1, rows], gate_w[1, cols, :])
            total += dot_nt(grad_hid[1, 0, rows], up_w[0, cols, :])
            total += dot_nt(grad_hid[1, 1, rows], up_w[1, cols, :])
            rows_in[0, labels[0] : labels[-1] + 1, :, :, cols] = total.reshape(
                len(labels), plane, capacity, STEP
            ).astype(jnp.bfloat16)

    def go_home(labels, c):
        for label in labels:
            start(home_copies(label, c))
            back_in[label, col, :, slab(c)] = rows_in[0, label, col, :, slab(c)]

    def relay_copy(label, c):
        return remote(
            back_in.at[label, :plane, :, slab(c)], back_in.at[label, plane:, :, slab(c)],
            b_send.at[label, c, 1, 0], b_recv.at[label, c, 1, 0], near_inner,
        )

    def relay(label):
        @pl.when(outer)
        def _():
            for c in pieces:
                arrived(home_copies(label, c))
                relay_copy(label, c).start()

    def homed(label, c):
        arrived(home_copies(label, c))
        if label != O:
            relay_copy(label, c).wait_recv()

    def combine(label, c, amount, extra, target, values):
        count = amount * capacity

        @pl.loop(c * piece // STEP, (c + 1) * piece // STEP)
        def _(k):
            cols = pl.ds(pl.multiple_of(k * STEP, STEP), STEP)
            rows = rows_of(back_in.at[label, :amount], cols)
            total = dot(mats[label, 0, :, :count], rows) + dot(mats[label, 1, :, :count], rows)
            if extra is not None:
                total += extra[:, cols].astype(jnp.float32)
            target[:, cols] = total.astype(jnp.bfloat16)

        if c == PIECES - 1:
            rows = rows_of(back_in.at[label, :amount], pl.ds(width, LANES))
            lane = lax.broadcasted_iota(jnp.int32, (LANES, LANES), 1)
            total = jnp.where(
                lane < LANES // 2,
                dot(mats[label, 2, :, :count], rows),
                dot(mats[label, 3, :, :count], rows),
            )
            if extra is not None:
                total += extra[:, width:].astype(jnp.float32)
            if values is None:
                half = LANES // 2
                row = lax.broadcasted_iota(jnp.int32, (8, LANES), 0)
                column = lax.broadcasted_iota(jnp.int32, (8, LANES), 1)
                first = jnp.where(column == row * half, 1.0, 0.0).astype(jnp.bfloat16)
                turned = dot_nt(first, total.astype(jnp.bfloat16))
                probs_out[...] = turned[:2].astype(jnp.bfloat16)
            else:
                values[...] = total.astype(jnp.bfloat16)

    def partial(which, c):
        return remote(
            land.at[1 + which, 0, :, slab(c)], part_in.at[which, :, slab(c)],
            p_send.at[which, c], p_recv.at[which, c], far_inner,
        )

    def last_hop(c):
        return remote(
            land.at[0, 0, :, slab(c)], land.at[0, 0, :, slab(c)], p_send.at[2, c], p_recv.at[2, c],
            near_outer,
        )

    def value_columns(ref):
        return ref.at[:, width:]

    parts, pieces, streams = range(PARTS), range(PIECES), range(2)

    @pl.when(inner)
    def _():
        tables(I, table[...], inner_base, outer_base, 2 * plane)

    @pl.when(outer)
    def _():
        tables(O, table[...], my_base, my_base, plane)

    for stream in streams:
        blocks[stream].wait()

        @pl.when(inner)
        def _():
            for i in parts:
                deal(I, stream, i, own.at[stream], stream, 0, 2 * plane)

        @pl.when(outer)
        def _():
            for i in parts:
                deal(O, stream, i, own.at[stream], stream, 0, plane)

    def own_sent():
        @pl.when(inner)
        def _():
            sent([up_table(1, far_inner)] + ups(1, far_inner))

    def cross_rest():
        @pl.when(inner)
        def _():
            for stream in streams:
                for i in parts:
                    if stream or i >= LEAD:
                        up_block(stream, i, 1, far_inner).start()

    def pass_outer(stream, some):
        @pl.when(inner)
        def _():
            for i in some:
                up_block(stream, i, 0, near_inner).wait_recv()
                pass_block(stream, i).start()
                deal(O, stream, i, land.at[0, stream], 4, stream * plane, plane)

    def deal_far(label, target, stream, buf, some):
        @pl.when(inner)
        def _():
            for i in some:
                up_block(stream, i, target, far_inner).wait_recv()
                deal(label, stream, i, land.at[target, stream], buf, 0, 2 * plane)

    def pass_and_deal():
        for i in parts:
            pass_outer(1, (i,))
            deal_far(FO, 2, 0, 2, (i,))

    def outer_tables():
        @pl.when(inner)
        def _():
            up_table(0, near_inner).wait_recv()
            pass_table().start()
            tables(O, far_table[0], my_base, my_base, plane)

    def far_tables(label):
        @pl.when(inner)
        def _():
            up_table(label - 1, far_inner).wait_recv()
            tables(label, far_table[label - 1], inner_base, outer_base, 2 * plane)

    def own_dealt():
        @pl.when(inner)
        def _():
            for stream in streams:
                for i in parts:
                    sent(deal_copies(I, stream, i, stream, 0) + deal_across(I, stream, i, stream))

    near = (I, O)

    def take_weights():
        for copy in locals_:
            copy.wait()
        arrived(swaps)

    def front(labels):
        for i in parts:
            for label in labels:
                dealt(label, 0, i)
            front_in(labels, i)

    def finish(labels):
        for i in parts:
            for label in labels:
                dealt(label, 1, i)
            front_out(labels, i)
        pointwise(labels)

    def make_home(labels):
        for c in pieces:
            home(labels, c)

    def start_home(labels):
        for c in pieces:
            go_home(labels, c)

    def send_home(labels):
        for c in pieces:
            home(labels, c)
            go_home(labels, c)

    def cross_back(label, which, some):
        @pl.when(inner)
        def _():
            target = land.at[1 + which, 0]
            for c in some:
                homed(label, c)
                combine(label, c, 2 * plane, None, target, value_columns(target))
                partial(which, c).start()

    def own_result():
        @pl.when(inner)
        def _():
            for c in pieces:
                homed(I, c)
                partial(0, c).wait_recv()
                combine(I, c, 2 * plane, part_in.at[0], out, None)

    def passed():
        @pl.when(inner)
        def _():
            for i in parts:
                pass_block(0, i).wait_send()

    def inward_result(some):
        @pl.when(inner)
        def _():
            for c in some:
                homed(O, c)
                partial(1, c).wait_recv()
                combine(O, c, plane, part_in.at[1], land.at[0, 0], value_columns(land.at[0, 0]))
                last_hop(c).start()

    def outer_result():
        @pl.when(outer)
        def _():
            for c in pieces:
                homed(O, c)
                last_hop(c).wait_recv()
                combine(O, c, plane, land.at[0, 0], out, None)

    def both_results():
        for c in pieces:
            inward_result((c,))
            cross_back(FI, 0, (c,))

    outer_tables()
    pass_outer(0, parts)
    far_tables(FO)
    pass_and_deal()
    cross_rest()
    deal_far(FO, 2, 1, 3, parts[:2])
    take_weights()
    front(near)
    deal_far(FO, 2, 1, 3, parts[2:])
    finish(near)
    make_home(near)
    start_home((O,))
    front((FO,))
    finish((FO,))
    send_home((FO,))
    far_tables(FI)
    own_dealt()
    deal_far(FI, 1, 0, 0, parts)
    relay(FO)
    front((FI,))
    start_home((I,))
    relay(I)
    deal_far(FI, 1, 1, 1, parts[:1])
    cross_back(FO, 1, pieces)
    deal_far(FI, 1, 1, 1, parts[1:])
    finish((FI,))
    send_home((FI,))
    relay(FI)
    passed()
    both_results()
    outer_result()
    own_result()
    own_sent()

    @pl.when(inner)
    def _():
        pass_table().wait_send()
        sent([pass_block(1, i) for i in parts])
        for stream in streams:
            for i in parts:
                sent(deal_copies(O, stream, i, 4, stream * plane))
                for label, buf in ((FI, 0), (FO, 2)):
                    sent(deal_copies(label, stream, i, buf + stream, 0))
                    sent(deal_across(label, stream, i, buf + stream))
        for c in pieces:
            for label in (I, FI, FO):
                sent(home_copies(label, c))
            sent([partial(0, c), partial(1, c), last_hop(c)])

    @pl.when(outer)
    def _():
        sent([up_table(0, near_inner)] + ups(0, near_inner))
        for stream in streams:
            for i in parts:
                sent(deal_copies(O, stream, i, stream, 0))
        for c in pieces:
            for label in (I, FI, FO):
                sent([*home_copies(label, c), relay_copy(label, c)])

    for c in pieces:
        sent(home_copies(O, c))
    sent(swaps)


def fused_on_device(tokens, routes, route_probs, gate_weight, up_weight, down_weight, grad_out):
    tok_count, width = tokens.shape
    top_count = routes.shape[1]
    experts = lax.axis_size("expert")
    capacity = 3 * tok_count * top_count // (2 * experts)
    plane = experts // LAYERS
    hid = gate_weight.shape[2]
    full = width + LANES
    bf16, f32 = jnp.bfloat16, jnp.float32
    vmem, sems = pltpu.VMEM, pltpu.SemaphoreType.DMA
    spec = pl.BlockSpec(memory_space=pltpu.VMEM)
    raw = pl.BlockSpec(memory_space=pl.ANY)
    grad_tokens, values = pl.pallas_call(
        lambda *refs: fused_kernel(plane, *refs),
        name="routed_backward",
        out_shape=(
            jax.ShapeDtypeStruct((tok_count, width), bf16),
            jax.ShapeDtypeStruct((top_count, tok_count), bf16),
        ),
        in_specs=[spec] * 2 + [raw] * 5,
        out_specs=(spec, spec),
        scratch_shapes=[
            vmem((8, tok_count), f32),
            vmem((2, tok_count, width), bf16),
            vmem((4, 2 * plane * capacity, tok_count), bf16),
            vmem((4, 4, tok_count, 2 * plane * capacity), bf16),
            vmem((3, 8, tok_count), f32),
            vmem((3, 2, tok_count, full), bf16),
            vmem((2, width, hid), bf16),
            vmem((2, width, hid), bf16),
            vmem((2, hid, width), bf16),
            vmem((5, 2 * plane, capacity, width), bf16),
            vmem((2, 4, plane, capacity, full), bf16),
            vmem((3, 2, 3 * plane * capacity, hid), f32),
            vmem((2, 2, 4 * plane * capacity, hid), bf16),
            vmem((4, 2 * plane, capacity, full), bf16),
            vmem((2, tok_count, full), bf16),
            sems((5,)),
            sems((3,)), sems((3,)),
            sems((2,)), sems((3,)),
            sems((2, 2, PARTS)), sems((3, 2, PARTS)),
            sems((4, 2, PARTS, 2, plane)), sems((4, 2, PARTS, plane)),
            sems((4, PIECES, 2, plane)), sems((4, PIECES, 2, plane)),
            sems((3, PIECES)), sems((3, PIECES)),
        ],
        compiler_params=pltpu.CompilerParams(
            collective_id=0, has_side_effects=True, vmem_limit_bytes=63 * 1024 * 1024
        ),
    )(routes.T, route_probs.T, tokens, grad_out, gate_weight, up_weight, down_weight)
    return grad_tokens, values.T


def on_device(tokens, routes, *rest):
    experts = lax.axis_size("expert")
    capacity = 3 * routes.shape[0] * routes.shape[1] // (2 * experts)
    fits = capacity % 8 == 0 and lax.axis_size("seq") == 2 and routes.shape[1] == 2
    fits = fits and experts == LAYERS * (experts // LAYERS) and routes.shape[0] == LANES
    run = fused_on_device if fits else halves_on_device
    return run(tokens, routes, *rest)


def solution(mesh):
    placed = (
        P(("seq", "expert"), None),
        P(("seq", "expert"), None),
        P(("seq", "expert"), None),
        P("expert", None, "seq"),
        P("expert", None, "seq"),
        P("expert", "seq", None),
        P(("seq", "expert"), None),
    )
    return jax.shard_map(
        on_device,
        mesh=mesh,
        in_specs=placed,
        out_specs=(P(("seq", "expert"), None), P(("seq", "expert"), None)),
        check_vma=False,
    )
```
